32 devices in a mesh: seq: 8 (over z, core), batch: 4 (over y, x).
Axes of the slice: x: 2, y: 2, z: 4, core: 2. Of those that a mesh axis runs over, the one named last changes fastest.
Arguments:
- inputs: bfloat16 [4, 64, 8192], P('batch'), may hold values from -6 to 6
- w_query: bfloat16 [8192, 8192], P('batch', 'seq'), may hold values from -0.0625 to 0.0625
- cache_keys: bfloat16 [4, 4096, 1024], P('batch', 'seq'), may hold values from -120 to 120
- cache_values: bfloat16 [4, 4096, 1024], P('batch', 'seq'), may hold values from -6 to 6
- lengths: int32 [4], P('batch'), may hold values from 1 to 4096, as said below
- positions: int32 [4, 64], P('batch'), may hold values from 0 to 4095, as said below
Outputs:
- attended: bfloat16 [4, 64, 8192], P('batch', None, 'seq')
The draws below stay inside these ranges and needn't reach their ends.
Inputs may be any that keep to these rules, and one draw needn't show every extreme that they name: `lengths`: every sample has at least one valid position; some sample has all 4096 valid. `positions`: some query sits at position 0 and some at 4095.
All inputs are finite; a program needn't handle non-finite values.
Results may differ from the reference program's by a relative error of at most 0.015.
The reference program's roundings to bfloat16 on the way (of `query`, `prob` and `block_sum`) count: a program that leaves them out, or rounds other values in their place, can miss the bound.
Values may be sent and summed in bfloat16 or wider, within the bound.
No kernel may reach another device: no remote copies, remote signals or barrier semaphores. Data moves between devices by JAX's collectives and lax.ppermute only.
A program may use at most 64 MiB of HBM per device.

```python
import jax
import jax.numpy as jnp
from jax import lax

D = 8192
H = 64
KVH = 8
HD = 128
Q = 64
SAMPLES = 4
S = 4096
N_SEQ = 8


def draw_cache_keys(key, part):
    shape = (SAMPLES, S, KVH * HD)
    base = jnp.clip(jax.random.normal(key, shape, jnp.float32), -4.0, 4.0)
    return base.astype(jnp.bfloat16)


def draw_lengths(key, part):
    first, second = jax.random.split(jax.random.fold_in(key, 11))
    drawn = jax.random.randint(first, (SAMPLES,), 1, S + 1)
    which = jax.random.randint(second, (), 0, SAMPLES)
    return drawn.at[which].set(S).astype(jnp.int32)


def draw_positions(key, part):
    drawn = jax.random.randint(jax.random.fold_in(key, 13), (SAMPLES, Q), 0, S)
    drawn = drawn.at[0, 0].set(0).at[SAMPLES - 1, Q - 1].set(S - 1)
    return drawn.astype(jnp.int32)


def steps_of(stream_key, shape, shards, low, high):
    loudness = 1.0
    for position, shards_of in shards:
        draws = jax.random.uniform(jax.random.fold_in(jax.random.fold_in(stream_key, 6), position), (shards_of,), jnp.float32, low / len(shards), high / len(shards))
        loudness = loudness * jnp.repeat(jnp.exp(draws), shape[position] // shards_of).reshape((-1,) + (1,) * (len(shape) - 1 - position))
    return loudness


def bell_draw(rng, shape, scale, reach, shards=(), held_as=jnp.bfloat16):
    level = steps_of(rng, shape, shards, -0.22, 0.18) if shards else 1.0
    array = jax.random.normal(rng, shape, jnp.float32) * scale * level
    return jnp.minimum(jnp.maximum(array, -reach), reach).astype(held_as)


def setup_inputs(seed: int = 0) -> dict:
    key_list = jax.random.split(jax.random.key(seed), 7)
    return {
        "inputs": bell_draw(key_list[0], (SAMPLES, Q, D), 1.0, 6.0, ((0, 4),)),
        "w_query": bell_draw(key_list[1], (D, H * HD), D ** -0.5, 0.0625, ((0, 4), (1, 8))),
        "cache_keys": draw_cache_keys(jax.random.fold_in(key_list[6], 71), 0),
        "cache_values": bell_draw(key_list[3], (SAMPLES, S, KVH * HD), 1.0, 6.0, ((0, 4), (1, 8))),
        "lengths": draw_lengths(jax.random.fold_in(key_list[6], 71), 0),
        "positions": draw_positions(jax.random.fold_in(key_list[6], 71), 0),
    }


def one_sample(w_query, args):
    tokens, key_rows, value_rows, length, place = args
    group = H // KVH
    block_len = S // N_SEQ
    query = jnp.dot(tokens, w_query, preferred_element_type=jnp.float32).astype(jnp.bfloat16)
    query_heads = query.reshape(Q, KVH, group, HD).astype(jnp.float32)
    key_blocks = key_rows.reshape(N_SEQ, block_len, KVH, HD)
    value_blocks = value_rows.reshape(N_SEQ, block_len, KVH, HD)

    def one_block(items):
        key_block, value_block, index = items
        key_pos = index * block_len + jnp.arange(block_len, dtype=jnp.int32)
        visible = (key_pos[None, :] <= place[:, None]) & (key_pos[None, :] < length)
        score = jnp.einsum('qgrd,kgd->grqk', query_heads, key_block.astype(jnp.float32)) * (HD ** -0.5)
        block_max = jnp.max(jnp.where(visible, score, -1e30), axis=-1)
        expo = jnp.where(visible, jnp.exp(score - block_max[..., None]), 0.0)
        block_total = jnp.sum(expo, axis=-1)
        prob = expo.astype(jnp.bfloat16).astype(jnp.float32)
        block_sum = jnp.einsum('grqk,kgd->grqd', prob, value_block.astype(jnp.float32)).astype(jnp.bfloat16)
        return block_sum.reshape(H, Q, HD), block_max.reshape(H, Q), block_total.reshape(H, Q)

    sums, maxima, totals = lax.map(one_block, (key_blocks, value_blocks, jnp.arange(N_SEQ, dtype=jnp.int32)))
    top = jnp.max(maxima, axis=0)
    weight = jnp.exp(maxima - top[None])
    numer = jnp.sum(weight[..., None] * sums.astype(jnp.float32), axis=0)
    denom = jnp.sum(weight * totals, axis=0)
    result = numer / denom[..., None]
    return jnp.transpose(result, (1, 0, 2)).reshape(Q, H * HD).astype(jnp.bfloat16)


def reference(inputs, w_query, cache_keys, cache_values, lengths, positions):
    def per_sample(args):
        return one_sample(w_query, args)

    return lax.map(per_sample, (inputs, cache_keys, cache_values, lengths, positions))
```

```python
import functools

import jax
import jax.numpy as jnp
from jax import lax
from jax.experimental import pallas as pl
from jax.experimental.pallas import tpu as pltpu
from jax.sharding import PartitionSpec as P

H = 64
KVH = 8
HD = 128


ANY = pl.BlockSpec(memory_space=pl.ANY)
VMEM = pl.BlockSpec(memory_space=pltpu.VMEM)
SMEM = pl.BlockSpec(memory_space=pltpu.SMEM)
LOG2E = 1.4426950408889634
NONE_VISIBLE = -1e30


def peers(count, step):
    if count & (count - 1) == 0:
        return [(j, j ^ step) for j in range(count)]
    return [(j, (j + step) % count) for j in range(count)]


def target(me, count, step):
    return me ^ step if count & (count - 1) == 0 else lax.rem(me + step, count)


def source(me, count, step):
    return me ^ step if count & (count - 1) == 0 else lax.rem(me + count - step, count)


def pack_cache(key_rows, value_rows, seq_count, steps):
    keys_here, width = key_rows.shape
    share = width // seq_count

    def kernel(keys, values, *rest):
        outs, sem = rest[:-1], rest[-1]
        me = lax.axis_index("seq")
        copies = []
        for n, step in enumerate(steps):
            columns = pl.ds(pl.multiple_of(target(me, seq_count, step) * share, share), share)
            for part, rows in enumerate((keys, values)):
                copy = pltpu.make_async_copy(rows.at[:, columns], outs[n].at[part], sem.at[n, part])
                copy.start()
                copies.append(copy)
        for copy in copies:
            copy.wait()

    return pl.pallas_call(
        kernel,
        out_shape=[jax.ShapeDtypeStruct((2, keys_here, share), key_rows.dtype)] * len(steps),
        in_specs=[ANY, ANY],
        out_specs=[VMEM] * len(steps),
        scratch_shapes=[pltpu.SemaphoreType.DMA((len(steps), 2))],
        cost_estimate=pl.CostEstimate(
            flops=0, transcendentals=0, bytes_accessed=len(steps) * 8 * keys_here * share
        ),
        name="pack_cache",
    )(key_rows, value_rows)


def pack_features(tokens, batch_count):
    rows, width = tokens.shape
    share = width // batch_count

    def kernel(tokens_ref, *rest):
        outs, sem = rest[:-1], rest[-1]
        me = lax.axis_index("batch")
        copies = []
        for step in range(batch_count):
            columns = pl.ds(pl.multiple_of(target(me, batch_count, step) * share, share), share)
            copy = pltpu.make_async_copy(tokens_ref.at[:, columns], outs[step], sem.at[step])
            copy.start()
            copies.append(copy)
        for copy in copies:
            copy.wait()

    return pl.pallas_call(
        kernel,
        out_shape=[jax.ShapeDtypeStruct((rows, share), tokens.dtype)] * batch_count,
        in_specs=[ANY],
        out_specs=[VMEM] * batch_count,
        scratch_shapes=[pltpu.SemaphoreType.DMA((batch_count,))],
        cost_estimate=pl.CostEstimate(flops=0, transcendentals=0, bytes_accessed=4 * rows * width),
        name="pack_features",
    )(tokens)


def project(blocks, weight):
    count = len(blocks)
    rows, depth = blocks[0].shape
    columns = weight.shape[1]
    tile = min(256, columns)

    def kernel(*refs):
        ins, w_ref, outs, stacked = refs[:count], refs[count], refs[count + 1 : -1], refs[-1]

        @pl.when(pl.program_id(0) == 0)
        def _():
            for n in range(count):
                stacked[pl.ds(n * rows, rows), :] = ins[n][...]

        product = jnp.dot(stacked[...], w_ref[...], preferred_element_type=jnp.float32)
        for n in range(count):
            outs[n][...] = product[n * rows : (n + 1) * rows]

    return pl.pallas_call(
        kernel,
        grid=(columns // tile,),
        out_shape=[jax.ShapeDtypeStruct((rows, columns), jnp.float32)] * count,
        in_specs=[pl.BlockSpec((rows, depth), lambda j: (0, 0))] * count
        + [pl.BlockSpec((depth, tile), lambda j: (0, j))],
        out_specs=[pl.BlockSpec((rows, tile), lambda j: (0, j))] * count,
        scratch_shapes=[pltpu.VMEM((count * rows, depth), blocks[0].dtype)],
        cost_estimate=pl.CostEstimate(
            flops=2 * count * rows * depth * columns,
            transcendentals=0,
            bytes_accessed=2 * depth * columns + 6 * count * rows * depth,
        ),
        name="project",
    )(*blocks, weight)


def attend(query, chunks, steps, state, positions, lengths, seq_count, last):
    first = state is None
    tokens = positions.shape[1]
    group = H // KVH
    columns = group * tokens
    n_query = len(query)
    n_chunks = len(chunks)
    keys_here = chunks[0].shape[-2]
    inputs = [lengths, positions, *query, *chunks] + ([] if first else list(state))
    state_shape = [
        jax.ShapeDtypeStruct((1, columns), jnp.float32),
        jax.ShapeDtypeStruct((1, columns), jnp.float32),
        jax.ShapeDtypeStruct((HD, columns), jnp.float32),
    ]
    if last:
        out_shape = [jax.ShapeDtypeStruct((tokens, group * HD), jnp.bfloat16)]
    else:
        out_shape = state_shape
        if first:
            out_shape = out_shape + [jax.ShapeDtypeStruct((columns, HD), jnp.bfloat16)]

    def kernel(*refs):
        lengths_ref, positions_ref = refs[:2]
        query_refs = refs[2 : 2 + n_query]
        chunk_refs = refs[2 + n_query : 2 + n_query + n_chunks]
        outs = refs[len(inputs) :]
        me = lax.axis_index("seq")
        if first:
            total = query_refs[0][...]
            for ref in query_refs[1:]:
                total = total + ref[...]
            rounded = total.astype(jnp.bfloat16)
            q = jnp.concatenate([rounded[:, h * HD : (h + 1) * HD] for h in range(group)], axis=0)
            if not last:
                outs[3][...] = q
            top = denom = numer = None
        else:
            q = query_refs[0][...]
            state_refs = refs[2 + n_query + n_chunks : len(inputs)]
            top, denom, numer = (ref[...] for ref in state_refs)
        limit = jnp.minimum(positions_ref[...], lengths_ref[0] - 1)
        limit = jnp.concatenate([limit] * group, axis=1)
        rows = lax.broadcasted_iota(jnp.int32, (keys_here, columns), 0)
        for ref, step in zip(chunk_refs, steps):
            start = source(me, seq_count, step) * keys_here
            score = lax.dot_general(
                ref[0], q, (((1,), (1,)), ((), ())), preferred_element_type=jnp.float32
            )
            score = jnp.where(rows <= limit - start, score, NONE_VISIBLE)
            block_max = jnp.max(score, axis=0, keepdims=True)
            expo = jnp.exp2((score - block_max) * (HD**-0.5 * LOG2E))
            block_total = jnp.sum(expo, axis=0, keepdims=True)
            block_sum = lax.dot_general(
                ref[1],
                expo.astype(jnp.bfloat16),
                (((0,), (0,)), ((), ())),
                preferred_element_type=jnp.float32,
            )
            block_sum = block_sum.astype(jnp.bfloat16).astype(jnp.float32)
            if top is None:
                top, denom, numer = block_max, block_total, block_sum
                continue
            new_top = jnp.maximum(top, block_max)
            keep = jnp.exp2((top - new_top) * (HD**-0.5 * LOG2E))
            weight = jnp.exp2((block_max - new_top) * (HD**-0.5 * LOG2E))
            denom = denom * keep + block_total * weight
            numer = numer * keep + block_sum * weight
            top = new_top
        if last:
            result = numer / denom
            for h in range(group):
                part = result[:, h * tokens : (h + 1) * tokens]
                outs[0][:, h * HD : (h + 1) * HD] = jnp.transpose(part).astype(jnp.bfloat16)
        else:
            outs[0][...] = top
            outs[1][...] = denom
            outs[2][...] = numer

    return pl.pallas_call(
        kernel,
        out_shape=out_shape,
        in_specs=[SMEM] + [VMEM] * (len(inputs) - 1),
        out_specs=[VMEM] * len(out_shape),
        cost_estimate=pl.CostEstimate(
            flops=4 * n_chunks * keys_here * columns * HD,
            transcendentals=n_chunks * keys_here * columns,
            bytes_accessed=n_chunks * 4 * keys_here * HD,
        ),
        name="attend",
    )(*inputs)


def own_heads(inputs, w_query, cache_keys, cache_values, lengths, positions):
    seq_count = lax.axis_size("seq")
    batch_count = lax.axis_size("batch")
    key_rows, value_rows, tokens = cache_keys[0], cache_values[0], inputs[0]
    order = list(range(1, seq_count))
    packed = pack_cache(key_rows, value_rows, seq_count, [*order, 0])
    moved = {
        step: lax.ppermute(block, "seq", peers(seq_count, step)) for step, block in zip(order, packed)
    }
    moved[0] = packed[-1]
    blocks = pack_features(tokens, batch_count)
    blocks = [blocks[0]] + [
        lax.ppermute(blocks[step], "batch", peers(batch_count, step)) for step in range(1, batch_count)
    ]
    partials = project(blocks, w_query)
    back = [partials[0]] + [
        lax.ppermute(partials[step], "batch", [(b, a) for a, b in peers(batch_count, step)])
        for step in range(1, batch_count)
    ]
    attend_ = functools.partial(
        attend, positions=positions, lengths=lengths, seq_count=seq_count
    )
    half = seq_count // 2
    early = list(range(half))
    middle, late = list(range(half, seq_count, 2)), list(range(half + 1, seq_count, 2))
    *state, query = attend_(back, [moved[s] for s in early], early, None, last=False)
    if middle:
        state = attend_([query], [moved[s] for s in middle], middle, state, last=False)
    (out,) = attend_([query], [moved[s] for s in late], late, state, last=True)
    return out[None]


def split_positions(inputs, w_query, cache_keys, cache_values, lengths, positions):
    seq_count = lax.axis_size("seq")
    heads_here = H // seq_count
    group = H // KVH
    keys_here = cache_keys.shape[1]
    tokens = inputs[0]
    query_rows = tokens.shape[0]
    features = lax.all_to_all(inputs, "batch", split_axis=2, concat_axis=0, tiled=True)
    query = lax.psum_scatter(
        jnp.einsum("sqd,dc->sqc", features, w_query, preferred_element_type=jnp.float32),
        "batch",
        scatter_dimension=0,
        tiled=True,
    )[0]
    query = query.astype(jnp.bfloat16)
    all_query = lax.all_gather(query, "seq", axis=1, tiled=True)
    query_heads = all_query.reshape(query_rows, KVH, group, HD)
    key_pos = lax.axis_index("seq") * keys_here + jnp.arange(keys_here, dtype=jnp.int32)
    visible = (key_pos[None, :] <= positions[0][:, None]) & (key_pos[None, :] < lengths[0])
    key_rows = cache_keys[0]
    value_rows = cache_values[0]

    def one_head(kv_head):
        key_block = lax.dynamic_slice_in_dim(key_rows, kv_head * HD, HD, 1)
        value_block = lax.dynamic_slice_in_dim(value_rows, kv_head * HD, HD, 1)
        query_group = lax.dynamic_index_in_dim(query_heads, kv_head, 1, keepdims=False)
        score = jnp.einsum(
            "qrd,kd->rqk", query_group, key_block, preferred_element_type=jnp.float32
        ) * HD ** (-0.5)
        block_max = jnp.max(jnp.where(visible[None], score, -1e30), axis=-1)
        expo = jnp.where(visible[None], jnp.exp(score - block_max[..., None]), 0.0)
        block_total = jnp.sum(expo, axis=-1)
        prob = expo.astype(jnp.bfloat16)
        block_sum = jnp.einsum(
            "rqk,kd->rqd", prob, value_block, preferred_element_type=jnp.float32
        ).astype(jnp.bfloat16)
        return (block_sum, block_max, block_total)

    sums, maxima, totals = lax.map(one_head, jnp.arange(KVH, dtype=jnp.int32))
    sums = sums.reshape(1, H, query_rows, HD)
    maxima = maxima.reshape(1, H, query_rows)
    totals = totals.reshape(1, H, query_rows)
    got_sums = lax.all_to_all(sums, "seq", split_axis=1, concat_axis=0, tiled=True)
    got_max, got_total = (
        lax.all_to_all(maxima, "seq", split_axis=1, concat_axis=0, tiled=True),
        lax.all_to_all(totals, "seq", split_axis=1, concat_axis=0, tiled=True),
    )
    top = jnp.max(got_max, axis=0)
    weight = jnp.exp(got_max - top[None])
    numer = jnp.sum(weight[..., None] * got_sums.astype(jnp.float32), axis=0)
    denom = jnp.sum(weight * got_total, axis=0)
    result = numer / denom[..., None]
    return (
        jnp.transpose(result, (1, 0, 2))
        .reshape(query_rows, heads_here * HD)[None]
        .astype(jnp.bfloat16)
    )


def solution(mesh):
    in_specs = (
        P("batch", None, None),
        P("batch", "seq"),
        P("batch", "seq", None),
        P("batch", "seq", None),
        P("batch"),
        P("batch", None),
    )
    out_specs = P("batch", None, "seq")
    on_device = own_heads if mesh.shape["seq"] == KVH else split_positions
    return jax.shard_map(
        on_device, mesh=mesh, in_specs=in_specs, out_specs=out_specs, check_vma=False
    )
```

```python
import functools

import jax
import jax.numpy as jnp
from jax import lax
from jax.experimental import pallas as pl
from jax.experimental.pallas import tpu as pltpu
from jax.sharding import PartitionSpec as P


H = 64
KVH = 8
HD = 128


ANY = pl.BlockSpec(memory_space=pl.ANY)
HBM = pl.BlockSpec(memory_space=pltpu.HBM)
VMEM = pl.BlockSpec(memory_space=pltpu.VMEM)
SMEM = pl.BlockSpec(memory_space=pltpu.SMEM)
SMALL = pltpu.CompilerParams(vmem_limit_bytes=24 << 20)
LOG2E = 1.4426950408889634
NONE_VISIBLE = -1e30


def peers(count, step):
    if count & (count - 1) == 0:
        return [(j, j ^ step) for j in range(count)]
    return [(j, (j + step) % count) for j in range(count)]


def target(me, count, step):
    return me ^ step if count & (count - 1) == 0 else lax.rem(me + step, count)


def source(me, count, step):
    return me ^ step if count & (count - 1) == 0 else lax.rem(me + count - step, count)


def seq_order(count):
    half = count // 2
    far = [*range(half + 2, count, 2), *range(half + 1, count, 2)]
    return [half, *range(2, half), *far, 1]


def pack_cache(key_rows, value_rows, seq_count, steps):
    keys_here, width = key_rows.shape
    share = width // seq_count

    def kernel(keys, values, *rest):
        outs, sem = rest[:-1], rest[-1]
        me = lax.axis_index("seq")
        copies = []
        for n, step in enumerate(steps):
            columns = pl.ds(pl.multiple_of(target(me, seq_count, step) * share, share), share)
            for part, rows in enumerate((keys, values)):
                copy = pltpu.make_async_copy(rows.at[:, columns], outs[n].at[part], sem.at[n, part])
                copy.start()
                copies.append(copy)
        for copy in copies:
            copy.wait()

    return pl.pallas_call(
        kernel,
        out_shape=[jax.ShapeDtypeStruct((2, keys_here, share), key_rows.dtype)] * len(steps),
        in_specs=[HBM, HBM],
        out_specs=[VMEM] * len(steps),
        scratch_shapes=[pltpu.SemaphoreType.DMA((len(steps), 2))],
        cost_estimate=pl.CostEstimate(
            flops=0, transcendentals=0, bytes_accessed=len(steps) * 8 * keys_here * share
        ),
        compiler_params=SMALL,
        name="pack_cache",
    )(key_rows, value_rows)


def pack_features(tokens, batch_count):
    rows, width = tokens.shape
    share = width // batch_count

    def kernel(tokens_ref, *rest):
        outs, sem = rest[:-1], rest[-1]
        me = lax.axis_index("batch")
        copies = []
        for step in range(batch_count):
            columns = pl.ds(pl.multiple_of(target(me, batch_count, step) * share, share), share)
            copy = pltpu.make_async_copy(tokens_ref.at[:, columns], outs[step], sem.at[step])
            copy.start()
            copies.append(copy)
        for copy in copies:
            copy.wait()

    return pl.pallas_call(
        kernel,
        out_shape=[jax.ShapeDtypeStruct((rows, share), tokens.dtype)] * batch_count,
        in_specs=[HBM],
        out_specs=[VMEM] * batch_count,
        scratch_shapes=[pltpu.SemaphoreType.DMA((batch_count,))],
        cost_estimate=pl.CostEstimate(flops=0, transcendentals=0, bytes_accessed=4 * rows * width),
        compiler_params=SMALL,
        name="pack_features",
    )(tokens)


def project(blocks, weight):
    count = len(blocks)
    rows, depth = blocks[0].shape
    columns = weight.shape[1]
    tile = min(256, columns)

    def kernel(*refs):
        ins, w_ref, outs, stacked = refs[:count], refs[count], refs[count + 1 : -1], refs[-1]

        @pl.when(pl.program_id(0) == 0)
        def _():
            for n in range(count):
                stacked[pl.ds(n * rows, rows), :] = ins[n][...]

        product = jnp.dot(stacked[...], w_ref[...], preferred_element_type=jnp.float32)
        for n in range(count):
            outs[n][...] = product[n * rows : (n + 1) * rows]

    return pl.pallas_call(
        kernel,
        grid=(columns // tile,),
        out_shape=[jax.ShapeDtypeStruct((rows, columns), jnp.float32)] * count,
        in_specs=[pl.BlockSpec((rows, depth), lambda j: (0, 0))] * count
        + [pl.BlockSpec((depth, tile), lambda j: (0, j))],
        out_specs=[pl.BlockSpec((rows, tile), lambda j: (0, j))] * count,
        scratch_shapes=[pltpu.VMEM((count * rows, depth), blocks[0].dtype)],
        cost_estimate=pl.CostEstimate(
            flops=2 * count * rows * depth * columns,
            transcendentals=0,
            bytes_accessed=2 * depth * columns + 6 * count * rows * depth,
        ),
        compiler_params=SMALL,
        name="project",
    )(*blocks, weight)


def attend(query, chunks, steps, state, positions, lengths, seq_count, last):
    first = state is None
    tokens = positions.shape[1]
    group = H // KVH
    columns = group * tokens
    n_query = len(query)
    n_chunks = len(chunks)
    keys_here = chunks[0].shape[-2]
    moved = [*query, *chunks]
    inputs = [lengths, positions, *moved] + ([] if first else list(state))
    state_shape = [
        jax.ShapeDtypeStruct((1, columns), jnp.float32),
        jax.ShapeDtypeStruct((1, columns), jnp.float32),
        jax.ShapeDtypeStruct((HD, columns), jnp.float32),
    ]
    if last:
        out_shape = [jax.ShapeDtypeStruct((tokens, group * HD), jnp.bfloat16)]
    else:
        out_shape = state_shape
        if first:
            out_shape = out_shape + [jax.ShapeDtypeStruct((columns, HD), jnp.bfloat16)]

    def kernel(*refs):
        lengths_ref, positions_ref = refs[:2]
        moved_refs = refs[2 : 2 + len(moved)]
        state_refs = refs[2 + len(moved) : len(inputs)]
        outs = refs[len(inputs) : len(inputs) + len(out_shape)]
        held = refs[len(inputs) + len(out_shape) : -1]
        sem = refs[-1]
        copies = [
            pltpu.make_async_copy(src, dst, sem.at[n]) for n, (src, dst) in enumerate(zip(moved_refs, held))
        ]
        for copy in copies:
            copy.start()
        me = lax.axis_index("seq")
        limit = jnp.minimum(positions_ref[...], lengths_ref[0] - 1)
        limit = jnp.concatenate([limit] * group, axis=1)
        rows = lax.broadcasted_iota(jnp.int32, (keys_here, columns), 0)
        for copy in copies[:n_query]:
            copy.wait()
        if first:
            total = held[0][...]
            for ref in held[1:n_query]:
                total = total + ref[...]
            rounded = total.astype(jnp.bfloat16)
            q = jnp.concatenate([rounded[:, h * HD : (h + 1) * HD] for h in range(group)], axis=0)
            if not last:
                outs[3][...] = q
            top = denom = numer = None
        else:
            q = held[0][...]
            top, denom, numer = (ref[...] for ref in state_refs)
        for n, step in enumerate(steps):
            start = source(me, seq_count, step) * keys_here
            copies[n_query + n].wait()
            ref = held[n_query + n]
            score = lax.dot_general(
                ref[0], q, (((1,), (1,)), ((), ())), preferred_element_type=jnp.float32
            )
            score = jnp.where(rows <= limit - start, score, NONE_VISIBLE)
            block_max = jnp.max(score, axis=0, keepdims=True)
            expo = jnp.exp2((score - block_max) * (HD**-0.5 * LOG2E))
            block_total = jnp.sum(expo, axis=0, keepdims=True)
            block_sum = lax.dot_general(
                ref[1],
                expo.astype(jnp.bfloat16),
                (((0,), (0,)), ((), ())),
                preferred_element_type=jnp.float32,
            )
            block_sum = block_sum.astype(jnp.bfloat16).astype(jnp.float32)
            if top is None:
                top, denom, numer = block_max, block_total, block_sum
                continue
            new_top = jnp.maximum(top, block_max)
            keep = jnp.exp2((top - new_top) * (HD**-0.5 * LOG2E))
            weight = jnp.exp2((block_max - new_top) * (HD**-0.5 * LOG2E))
            denom = denom * keep + block_total * weight
            numer = numer * keep + block_sum * weight
            top = new_top
        if last:
            result = numer / denom
            for h in range(group):
                part = result[:, h * tokens : (h + 1) * tokens]
                outs[0][:, h * HD : (h + 1) * HD] = jnp.transpose(part).astype(jnp.bfloat16)
        else:
            outs[0][...] = top
            outs[1][...] = denom
            outs[2][...] = numer

    return pl.pallas_call(
        kernel,
        out_shape=out_shape,
        in_specs=[SMEM, VMEM] + [ANY] * len(moved) + [VMEM] * (len(inputs) - 2 - len(moved)),
        out_specs=[VMEM] * len(out_shape),
        scratch_shapes=[pltpu.VMEM(x.shape, x.dtype) for x in moved]
        + [pltpu.SemaphoreType.DMA((len(moved),))],
        cost_estimate=pl.CostEstimate(
            flops=4 * n_chunks * keys_here * columns * HD,
            transcendentals=n_chunks * keys_here * columns,
            bytes_accessed=n_chunks * 4 * keys_here * HD,
        ),
        compiler_params=SMALL,
        name="attend",
    )(*inputs)


def own_heads(inputs, w_query, cache_keys, cache_values, lengths, positions):
    seq_count = lax.axis_size("seq")
    batch_count = lax.axis_size("batch")
    order = seq_order(seq_count)
    key_rows, value_rows, tokens = cache_keys[0], cache_values[0], inputs[0]
    packed = pack_cache(key_rows, value_rows, seq_count, order[:3])
    blocks = list(pack_features(tokens, batch_count))
    packed = [*packed, *pack_cache(key_rows, value_rows, seq_count, [*order[3:], 0])]
    moved = {0: packed[-1]}
    for step, block in zip(order, packed):
        moved[step] = lax.ppermute(block, "seq", peers(seq_count, step))
    for step in range(1, batch_count):
        blocks[step] = lax.ppermute(blocks[step], "batch", peers(batch_count, step))
    partials = project(blocks, w_query)
    back = [partials[0]]
    for step in range(1, batch_count):
        back.append(lax.ppermute(partials[step], "batch", [(b, a) for a, b in peers(batch_count, step)]))
    attend_ = functools.partial(attend, positions=positions, lengths=lengths, seq_count=seq_count)
    half = seq_count // 2
    early, middle, late = [*range(half), order[0]], order[half - 1 : -2], order[-2:-1]
    *state, query = attend_(back, [moved[s] for s in early], early, None, last=False)
    state = attend_([query], [moved[s] for s in middle], middle, state, last=False)
    (out,) = attend_([query], [moved[s] for s in late], late, state, last=True)
    return out[None]


def split_positions(inputs, w_query, cache_keys, cache_values, lengths, positions):
    seq_count = lax.axis_size("seq")
    heads_here = H // seq_count
    group = H // KVH
    keys_here = cache_keys.shape[1]
    tokens = inputs[0]
    query_rows = tokens.shape[0]
    features = lax.all_to_all(inputs, "batch", split_axis=2, concat_axis=0, tiled=True)
    query = lax.psum_scatter(
        jnp.einsum("sqd,dc->sqc", features, w_query, preferred_element_type=jnp.float32),
        "batch",
        scatter_dimension=0,
        tiled=True,
    )[0]
    query = query.astype(jnp.bfloat16)
    all_query = lax.all_gather(query, "seq", axis=1, tiled=True)
    query_heads = all_query.reshape(query_rows, KVH, group, HD)
    key_pos = lax.axis_index("seq") * keys_here + jnp.arange(keys_here, dtype=jnp.int32)
    visible = (key_pos[None, :] <= positions[0][:, None]) & (key_pos[None, :] < lengths[0])
    key_rows = cache_keys[0]
    value_rows = cache_values[0]

    def one_head(kv_head):
        key_block = lax.dynamic_slice_in_dim(key_rows, kv_head * HD, HD, 1)
        value_block = lax.dynamic_slice_in_dim(value_rows, kv_head * HD, HD, 1)
        query_group = lax.dynamic_index_in_dim(query_heads, kv_head, 1, keepdims=False)
        score = jnp.einsum(
            "qrd,kd->rqk", query_group, key_block, preferred_element_type=jnp.float32
        ) * HD ** (-0.5)
        block_max = jnp.max(jnp.where(visible[None], score, -1e30), axis=-1)
        expo = jnp.where(visible[None], jnp.exp(score - block_max[..., None]), 0.0)
        block_total = jnp.sum(expo, axis=-1)
        prob = expo.astype(jnp.bfloat16)
        block_sum = jnp.einsum(
            "rqk,kd->rqd", prob, value_block, preferred_element_type=jnp.float32
        ).astype(jnp.bfloat16)
        return (block_sum, block_max, block_total)

    sums, maxima, totals = lax.map(one_head, jnp.arange(KVH, dtype=jnp.int32))
    sums = sums.reshape(1, H, query_rows, HD)
    maxima = maxima.reshape(1, H, query_rows)
    totals = totals.reshape(1, H, query_rows)
    got_sums = lax.all_to_all(sums, "seq", split_axis=1, concat_axis=0, tiled=True)
    got_max, got_total = (
        lax.all_to_all(maxima, "seq", split_axis=1, concat_axis=0, tiled=True),
        lax.all_to_all(totals, "seq", split_axis=1, concat_axis=0, tiled=True),
    )
    top = jnp.max(got_max, axis=0)
    weight = jnp.exp(got_max - top[None])
    numer = jnp.sum(weight[..., None] * got_sums.astype(jnp.float32), axis=0)
    denom = jnp.sum(weight * got_total, axis=0)
    result = numer / denom[..., None]
    return (
        jnp.transpose(result, (1, 0, 2))
        .reshape(query_rows, heads_here * HD)[None]
        .astype(jnp.bfloat16)
    )


def solution(mesh):
    in_specs = (
        P("batch", None, None),
        P("batch", "seq"),
        P("batch", "seq", None),
        P("batch", "seq", None),
        P("batch"),
        P("batch", None),
    )
    out_specs = P("batch", None, "seq")
    split = functools.partial(
        jax.shard_map, mesh=mesh, in_specs=in_specs, out_specs=out_specs, check_vma=False
    )
    if mesh.shape["seq"] != KVH:
        return split(split_positions)
    return split(own_heads)
```

```python
import functools

import jax
import jax.numpy as jnp
from jax import lax
from jax.experimental import pallas as pl
from jax.experimental.pallas import tpu as pltpu
from jax.sharding import PartitionSpec as P


H = 64
KVH = 8
HD = 128


ANY = pl.BlockSpec(memory_space=pl.ANY)
HBM = pl.BlockSpec(memory_space=pltpu.HBM)
VMEM = pl.BlockSpec(memory_space=pltpu.VMEM)
SMEM = pl.BlockSpec(memory_space=pltpu.SMEM)
PARTNERS = 0
SMALL = pltpu.CompilerParams(vmem_limit_bytes=24 << 20)
LOG2E = 1.4426950408889634
NONE_VISIBLE = -1e30


def peers(count, step):
    if count & (count - 1) == 0:
        return [(j, j ^ step) for j in range(count)]
    return [(j, (j + step) % count) for j in range(count)]


def target(me, count, step):
    return me ^ step if count & (count - 1) == 0 else lax.rem(me + step, count)


def source(me, count, step):
    return me ^ step if count & (count - 1) == 0 else lax.rem(me + count - step, count)


def seq_order(count):
    half = count // 2
    far = [*range(half + 2, count, 2), *range(half + 1, count, 2)]
    return [half, *range(2, half), *far, 1]


def pack_cache(key_rows, value_rows, seq_count, steps):
    keys_here, width = key_rows.shape
    share = width // seq_count

    def kernel(keys, values, *rest):
        outs, sem = rest[:-1], rest[-1]
        me = lax.axis_index("seq")
        copies = []
        for n, step in enumerate(steps):
            columns = pl.ds(pl.multiple_of(target(me, seq_count, step) * share, share), share)
            for part, rows in enumerate((keys, values)):
                copy = pltpu.make_async_copy(rows.at[:, columns], outs[n].at[part], sem.at[n, part])
                copy.start()
                copies.append(copy)
        for copy in copies:
            copy.wait()

    return pl.pallas_call(
        kernel,
        out_shape=[jax.ShapeDtypeStruct((2, keys_here, share), key_rows.dtype)] * len(steps),
        in_specs=[HBM, HBM],
        out_specs=[VMEM] * len(steps),
        scratch_shapes=[pltpu.SemaphoreType.DMA((len(steps), 2))],
        cost_estimate=pl.CostEstimate(
            flops=0, transcendentals=0, bytes_accessed=len(steps) * 8 * keys_here * share
        ),
        compiler_params=SMALL,
        name="pack_cache",
    )(key_rows, value_rows)


def pack_features(tokens, batch_count):
    rows, width = tokens.shape
    share = width // batch_count

    def kernel(tokens_ref, *rest):
        outs, sem = rest[:-1], rest[-1]
        me = lax.axis_index("batch")
        copies = []
        for step in range(batch_count):
            columns = pl.ds(pl.multiple_of(target(me, batch_count, step) * share, share), share)
            copy = pltpu.make_async_copy(tokens_ref.at[:, columns], outs[step], sem.at[step])
            copy.start()
            copies.append(copy)
        for copy in copies:
            copy.wait()

    return pl.pallas_call(
        kernel,
        out_shape=[jax.ShapeDtypeStruct((rows, share), tokens.dtype)] * batch_count,
        in_specs=[HBM],
        out_specs=[VMEM] * batch_count,
        scratch_shapes=[pltpu.SemaphoreType.DMA((batch_count,))],
        cost_estimate=pl.CostEstimate(flops=0, transcendentals=0, bytes_accessed=4 * rows * width),
        compiler_params=SMALL,
        name="pack_features",
    )(tokens)


def project(blocks, weight):
    count = len(blocks)
    rows, depth = blocks[0].shape
    columns = weight.shape[1]
    tile = min(256, columns)

    def kernel(*refs):
        ins, w_ref, outs, stacked = refs[:count], refs[count], refs[count + 1 : -1], refs[-1]

        @pl.when(pl.program_id(0) == 0)
        def _():
            for n in range(count):
                stacked[pl.ds(n * rows, rows), :] = ins[n][...]

        product = jnp.dot(stacked[...], w_ref[...], preferred_element_type=jnp.float32)
        for n in range(count):
            outs[n][...] = product[n * rows : (n + 1) * rows]

    return pl.pallas_call(
        kernel,
        grid=(columns // tile,),
        out_shape=[jax.ShapeDtypeStruct((rows, columns), jnp.float32)] * count,
        in_specs=[pl.BlockSpec((rows, depth), lambda j: (0, 0))] * count
        + [pl.BlockSpec((depth, tile), lambda j: (0, j))],
        out_specs=[pl.BlockSpec((rows, tile), lambda j: (0, j))] * count,
        scratch_shapes=[pltpu.VMEM((count * rows, depth), blocks[0].dtype)],
        cost_estimate=pl.CostEstimate(
            flops=2 * count * rows * depth * columns,
            transcendentals=0,
            bytes_accessed=2 * depth * columns + 6 * count * rows * depth,
        ),
        compiler_params=SMALL,
        name="project",
    )(*blocks, weight)


def swapped(me, pairs):
    other = me
    for one, two in pairs:
        other = jnp.where(me == one, two, jnp.where(me == two, one, other))
    return other


def round_query(partials):
    tokens, width = partials[0].shape
    group = width // HD

    def kernel(*refs):
        ins, out, held, sem = refs[: len(partials)], refs[len(partials)], refs[len(partials) + 1 : -1], refs[-1]
        copies = [pltpu.make_async_copy(src, dst, sem.at[n]) for n, (src, dst) in enumerate(zip(ins, held))]
        for copy in copies:
            copy.start()
        for copy in copies:
            copy.wait()
        for h in range(group):
            head = slice(h * HD, (h + 1) * HD)
            total = held[0][:, head]
            for ref in held[1:]:
                total = total + ref[:, head]
            out[h * tokens : (h + 1) * tokens, :] = total.astype(jnp.bfloat16)

    return pl.pallas_call(
        kernel,
        out_shape=jax.ShapeDtypeStruct((group * tokens, HD), jnp.bfloat16),
        in_specs=[ANY] * len(partials),
        out_specs=VMEM,
        scratch_shapes=[pltpu.VMEM(x.shape, x.dtype) for x in partials]
        + [pltpu.SemaphoreType.DMA((len(partials),))],
        cost_estimate=pl.CostEstimate(
            flops=len(partials) * tokens * width,
            transcendentals=0,
            bytes_accessed=4 * len(partials) * tokens * width,
        ),
        compiler_params=SMALL,
        name="round_query",
    )(*partials)


def merge(top, denom, numer, other_top, other_denom, other_numer):
    new_top = jnp.maximum(top, other_top)
    keep = jnp.exp2((top - new_top) * (HD**-0.5 * LOG2E))
    weight = jnp.exp2((other_top - new_top) * (HD**-0.5 * LOG2E))
    return new_top, denom * keep + other_denom * weight, numer * keep + other_numer * weight


def read_state(ref):
    return ref[HD : HD + 1, :], ref[HD + 8 : HD + 9, :], ref[:HD, :]


def attend(queries, chunks, steps, state, positions, lengths, seq_count, pairs):
    first = state is None
    tokens = positions.shape[1]
    columns = queries[0].shape[0]
    n_query = len(queries)
    n_chunks = len(chunks)
    keys_here = chunks[0].shape[-2]
    moved = [*queries, *chunks]
    inputs = [lengths, positions, *moved] + ([] if first else [state])

    def kernel(*refs):
        lengths_ref, positions_ref = refs[:2]
        moved_refs = refs[2 : 2 + len(moved)]
        out = refs[len(inputs)]
        held = refs[len(inputs) + 1 : -1]
        sem = refs[-1]
        copies = [
            pltpu.make_async_copy(src, dst, sem.at[n]) for n, (src, dst) in enumerate(zip(moved_refs, held))
        ]
        for copy in copies:
            copy.start()
        me = lax.axis_index("seq")
        other = swapped(me, pairs)
        limit = jnp.minimum(positions_ref[...], lengths_ref[0] - 1)
        limit = jnp.concatenate([limit] * (columns // tokens), axis=1)
        rows = lax.broadcasted_iota(jnp.int32, (keys_here, columns), 0)
        for copy in copies[:n_query]:
            copy.wait()
        q = held[0][...]
        if n_query == 2:
            q = jnp.where(other == me, q, held[1][...])
        sums = None if first else read_state(refs[len(inputs) - 1])
        for n, step in enumerate(steps):
            start = source(other, seq_count, step) * keys_here
            copies[n_query + n].wait()
            ref = held[n_query + n]
            score = lax.dot_general(
                ref[0], q, (((1,), (1,)), ((), ())), preferred_element_type=jnp.float32
            )
            score = jnp.where(rows <= limit - start, score, NONE_VISIBLE)
            block_max = jnp.max(score, axis=0, keepdims=True)
            expo = jnp.exp2((score - block_max) * (HD**-0.5 * LOG2E))
            block_total = jnp.sum(expo, axis=0, keepdims=True)
            block_sum = lax.dot_general(
                ref[1],
                expo.astype(jnp.bfloat16),
                (((0,), (0,)), ((), ())),
                preferred_element_type=jnp.float32,
            )
            block_sum = block_sum.astype(jnp.bfloat16).astype(jnp.float32)
            block = block_max, block_total, block_sum
            sums = block if sums is None else merge(*sums, *block)
        top, denom, numer = sums
        out[:HD, :] = numer
        out[HD : HD + 8, :] = jnp.broadcast_to(top, (8, columns))
        out[HD + 8 :, :] = jnp.broadcast_to(denom, (8, columns))

    return pl.pallas_call(
        kernel,
        out_shape=jax.ShapeDtypeStruct((HD + 16, columns), jnp.float32),
        in_specs=[SMEM, VMEM] + [ANY] * len(moved) + [VMEM] * (len(inputs) - 2 - len(moved)),
        out_specs=VMEM,
        scratch_shapes=[pltpu.VMEM(x.shape, x.dtype) for x in moved]
        + [pltpu.SemaphoreType.DMA((len(moved),))],
        cost_estimate=pl.CostEstimate(
            flops=4 * n_chunks * keys_here * columns * HD,
            transcendentals=n_chunks * keys_here * columns,
            bytes_accessed=n_chunks * 4 * keys_here * HD,
        ),
        compiler_params=SMALL,
        name="attend",
    )(*inputs)


def finish(near, far, received, tokens, pairs):
    columns = near.shape[1]
    group = columns // tokens

    def kernel(near_ref, far_ref, received_ref, out):
        me = lax.axis_index("seq")
        mine = swapped(me, pairs) == me
        far_sums = [
            jnp.where(mine, one, two) for one, two in zip(read_state(far_ref), read_state(received_ref))
        ]
        _, denom, numer = merge(*read_state(near_ref), *far_sums)
        result = numer / denom
        for h in range(group):
            part = result[:, h * tokens : (h + 1) * tokens]
            out[:, h * HD : (h + 1) * HD] = jnp.transpose(part).astype(jnp.bfloat16)

    return pl.pallas_call(
        kernel,
        out_shape=jax.ShapeDtypeStruct((tokens, group * HD), jnp.bfloat16),
        in_specs=[VMEM] * 3,
        out_specs=VMEM,
        cost_estimate=pl.CostEstimate(
            flops=8 * HD * columns, transcendentals=0, bytes_accessed=12 * HD * columns
        ),
        compiler_params=SMALL,
        name="finish",
    )(near, far, received)


def partner_pairs(count):
    half = count // 2
    across = half + half // 2
    return [(one, one ^ across) for one in range(half // 2, half)][:PARTNERS]


def own_heads(inputs, w_query, cache_keys, cache_values, lengths, positions):
    seq_count = lax.axis_size("seq")
    batch_count = lax.axis_size("batch")
    half = seq_count // 2
    order = seq_order(seq_count)
    pairs = partner_pairs(seq_count)
    meet = [*pairs, *((two, one) for one, two in pairs)]
    swap = dict(meet)
    key_rows, value_rows, tokens = (
        pltpu.with_memory_space_constraint(x[0], pltpu.HBM) for x in (cache_keys, cache_values, inputs)
    )
    blocks = list(pack_features(tokens, batch_count))
    packed = pack_cache(key_rows, value_rows, seq_count, order[:1])
    packed = [*packed, *pack_cache(key_rows, value_rows, seq_count, [*order[1:], 0])]
    moved = {0: packed[-1]}
    for step, block in zip(order, packed):
        to = peers(seq_count, step)
        if step >= half:
            to = [(a, swap.get(b, b)) for a, b in to]
        moved[step] = lax.ppermute(block, "seq", to)
    for step in range(1, batch_count):
        blocks[step] = lax.ppermute(blocks[step], "batch", peers(batch_count, step))
    partials = project(blocks, pltpu.with_memory_space_constraint(w_query, pltpu.HBM))
    back = [partials[0]]
    for step in range(1, batch_count):
        back.append(lax.ppermute(partials[step], "batch", [(b, a) for a, b in peers(batch_count, step)]))
    query = round_query(back)
    queries = [query]
    if pairs:
        queries.append(lax.ppermute(query, "seq", meet))
    attend_ = functools.partial(attend, positions=positions, lengths=lengths, seq_count=seq_count)
    early, middle, late = [*range(half)], [order[0], order[half - 1]], order[half:-1]
    near = attend_([query], [moved[s] for s in early], early, None, pairs=[])
    far = None
    for steps in (middle, late[:1], late[1:]):
        far = attend_(queries, [moved[s] for s in steps], steps, far, pairs=pairs)
    received = far
    if pairs:
        received = lax.ppermute(far, "seq", meet)
    return finish(near, far, received, positions.shape[1], pairs)[None]


def split_positions(inputs, w_query, cache_keys, cache_values, lengths, positions):
    seq_count = lax.axis_size("seq")
    heads_here = H // seq_count
    group = H // KVH
    keys_here = cache_keys.shape[1]
    tokens = inputs[0]
    query_rows = tokens.shape[0]
    features = lax.all_to_all(inputs, "batch", split_axis=2, concat_axis=0, tiled=True)
    query = lax.psum_scatter(
        jnp.einsum("sqd,dc->sqc", features, w_query, preferred_element_type=jnp.float32),
        "batch",
        scatter_dimension=0,
        tiled=True,
    )[0]
    query = query.astype(jnp.bfloat16)
    all_query = lax.all_gather(query, "seq", axis=1, tiled=True)
    query_heads = all_query.reshape(query_rows, KVH, group, HD)
    key_pos = lax.axis_index("seq") * keys_here + jnp.arange(keys_here, dtype=jnp.int32)
    visible = (key_pos[None, :] <= positions[0][:, None]) & (key_pos[None, :] < lengths[0])
    key_rows = cache_keys[0]
    value_rows = cache_values[0]

    def one_head(kv_head):
        key_block = lax.dynamic_slice_in_dim(key_rows, kv_head * HD, HD, 1)
        value_block = lax.dynamic_slice_in_dim(value_rows, kv_head * HD, HD, 1)
        query_group = lax.dynamic_index_in_dim(query_heads, kv_head, 1, keepdims=False)
        score = jnp.einsum(
            "qrd,kd->rqk", query_group, key_block, preferred_element_type=jnp.float32
        ) * HD ** (-0.5)
        block_max = jnp.max(jnp.where(visible[None], score, -1e30), axis=-1)
        expo = jnp.where(visible[None], jnp.exp(score - block_max[..., None]), 0.0)
        block_total = jnp.sum(expo, axis=-1)
        prob = expo.astype(jnp.bfloat16)
        block_sum = jnp.einsum(
            "rqk,kd->rqd", prob, value_block, preferred_element_type=jnp.float32
        ).astype(jnp.bfloat16)
        return (block_sum, block_max, block_total)

    sums, maxima, totals = lax.map(one_head, jnp.arange(KVH, dtype=jnp.int32))
    sums = sums.reshape(1, H, query_rows, HD)
    maxima = maxima.reshape(1, H, query_rows)
    totals = totals.reshape(1, H, query_rows)
    got_sums = lax.all_to_all(sums, "seq", split_axis=1, concat_axis=0, tiled=True)
    got_max, got_total = (
        lax.all_to_all(maxima, "seq", split_axis=1, concat_axis=0, tiled=True),
        lax.all_to_all(totals, "seq", split_axis=1, concat_axis=0, tiled=True),
    )
    top = jnp.max(got_max, axis=0)
    weight = jnp.exp(got_max - top[None])
    numer = jnp.sum(weight[..., None] * got_sums.astype(jnp.float32), axis=0)
    denom = jnp.sum(weight * got_total, axis=0)
    result = numer / denom[..., None]
    return (
        jnp.transpose(result, (1, 0, 2))
        .reshape(query_rows, heads_here * HD)[None]
        .astype(jnp.bfloat16)
    )


def solution(mesh):
    in_specs = (
        P("batch", None, None),
        P("batch", "seq"),
        P("batch", "seq", None),
        P("batch", "seq", None),
        P("batch"),
        P("batch", None),
    )
    out_specs = P("batch", None, "seq")
    split = functools.partial(
        jax.shard_map, mesh=mesh, in_specs=in_specs, out_specs=out_specs, check_vma=False
    )
    if mesh.shape["seq"] != KVH:
        return split(split_positions)
    return split(own_heads)
```

```python
import functools

import jax
import jax.numpy as jnp
from jax import lax
from jax.experimental import pallas as pl
from jax.experimental.pallas import tpu as pltpu
from jax.sharding import PartitionSpec as P


H = 64
KVH = 8
HD = 128


ANY = pl.BlockSpec(memory_space=pl.ANY)
HBM = pl.BlockSpec(memory_space=pltpu.HBM)
VMEM = pl.BlockSpec(memory_space=pltpu.VMEM)
SMEM = pl.BlockSpec(memory_space=pltpu.SMEM)
PARTNERS = 2
SMALL = pltpu.CompilerParams(vmem_limit_bytes=24 << 20)
LOG2E = 1.4426950408889634
NONE_VISIBLE = -1e30


def peers(count, step):
    if count & (count - 1) == 0:
        return [(j, j ^ step) for j in range(count)]
    return [(j, (j + step) % count) for j in range(count)]


def target(me, count, step):
    return me ^ step if count & (count - 1) == 0 else lax.rem(me + step, count)


def source(me, count, step):
    return me ^ step if count & (count - 1) == 0 else lax.rem(me + count - step, count)


def seq_order(count):
    half = count // 2
    far = [*range(half + 2, count, 2), *range(half + 1, count, 2)]
    return [half, *range(2, half), *far, 1]


def pack(key_rows, value_rows, tokens, seq_count, batch_count, steps):
    keys_here, width = key_rows.shape
    share = width // seq_count
    sources = [key_rows, value_rows] + ([] if tokens is None else [tokens])
    shapes = [jax.ShapeDtypeStruct((2, keys_here, share), key_rows.dtype)] * len(steps)
    if tokens is not None:
        depth = tokens.shape[1] // batch_count
        widths = [depth] + [depth // 2] * (batch_count - 1)
        shapes = shapes + [jax.ShapeDtypeStruct((tokens.shape[0], width), tokens.dtype) for width in widths]

    def kernel(*refs):
        ins, outs, sem = refs[: len(sources)], refs[len(sources) : -1], refs[-1]
        copies = []

        def move(ref, start, size, out):
            columns = pl.ds(pl.multiple_of(start, HD), size)
            copy = pltpu.make_async_copy(ref.at[:, columns], out, sem.at[len(copies)])
            copy.start()
            copies.append(copy)

        if tokens is not None:
            me, half = lax.axis_index("batch"), lax.rem(lax.axis_index("seq"), 2)
            for step, width in enumerate(widths):
                start = target(me, batch_count, step) * depth + (half * width if step else 0)
                move(ins[2], start, width, outs[len(steps) + step])
        me = lax.axis_index("seq")
        for n, step in enumerate(steps):
            for part in range(2):
                move(ins[part], target(me, seq_count, step) * share, share, outs[n].at[part])
        for copy in copies:
            copy.wait()

    n_copies = 2 * len(steps) + (0 if tokens is None else batch_count)
    out = pl.pallas_call(
        kernel,
        out_shape=shapes,
        in_specs=[HBM] * len(sources),
        out_specs=[VMEM] * len(shapes),
        scratch_shapes=[pltpu.SemaphoreType.DMA((n_copies,))],
        cost_estimate=pl.CostEstimate(
            flops=0, transcendentals=0, bytes_accessed=len(steps) * 8 * keys_here * share
        ),
        compiler_params=SMALL,
    )(*sources)
    return list(out)


def project(own, halves, other_halves, weight):
    count = 1 + len(halves)
    rows, depth = own.shape
    columns = weight.shape[1]
    tile = min(256, columns)

    def kernel(*refs):
        ins, w_ref, outs, stacked = refs[: 2 * count - 1], refs[2 * count - 1], refs[2 * count : -1], refs[-1]

        @pl.when(pl.program_id(0) == 0)
        def _():
            mine = lax.rem(lax.axis_index("seq"), 2)
            stacked[:rows, :] = ins[0][...]
            for n in range(1, count):
                for which, ref in ((mine, ins[n]), (1 - mine, ins[count - 1 + n])):
                    start = pl.multiple_of(which * (depth // 2), HD)
                    stacked[n * rows : (n + 1) * rows, pl.ds(start, depth // 2)] = ref[...]

        product = jnp.dot(stacked[...], w_ref[...], preferred_element_type=jnp.float32)
        for n in range(count):
            outs[n][...] = product[n * rows : (n + 1) * rows]

    return pl.pallas_call(
        kernel,
        grid=(columns // tile,),
        out_shape=[jax.ShapeDtypeStruct((rows, columns), jnp.float32)] * count,
        in_specs=[pl.BlockSpec((rows, depth), lambda j: (0, 0))]
        + [pl.BlockSpec((rows, depth // 2), lambda j: (0, 0))] * (2 * count - 2)
        + [pl.BlockSpec((depth, tile), lambda j: (0, j))],
        out_specs=[pl.BlockSpec((rows, tile), lambda j: (0, j))] * count,
        scratch_shapes=[pltpu.VMEM((count * rows, depth), own.dtype)],
        cost_estimate=pl.CostEstimate(
            flops=2 * count * rows * depth * columns,
            transcendentals=0,
            bytes_accessed=2 * depth * columns + 6 * count * rows * depth,
        ),
        compiler_params=SMALL,
        name="project",
    )(own, *halves, *other_halves, weight)


def swapped(me, pairs):
    other = me
    for one, two in pairs:
        other = jnp.where(me == one, two, jnp.where(me == two, one, other))
    return other


def round_query(partials):
    tokens, width = partials[0].shape
    group = width // HD

    def kernel(*refs):
        ins, out, held, sem = refs[: len(partials)], refs[len(partials)], refs[len(partials) + 1 : -1], refs[-1]
        copies = [pltpu.make_async_copy(src, dst, sem.at[n]) for n, (src, dst) in enumerate(zip(ins, held))]
        for copy in copies:
            copy.start()
        for copy in copies:
            copy.wait()
        for h in range(group):
            head = slice(h * HD, (h + 1) * HD)
            total = held[0][:, head]
            for ref in held[1:]:
                total = total + ref[:, head]
            out[h * tokens : (h + 1) * tokens, :] = total.astype(jnp.bfloat16)

    return pl.pallas_call(
        kernel,
        out_shape=jax.ShapeDtypeStruct((group * tokens, HD), jnp.bfloat16),
        in_specs=[ANY] * len(partials),
        out_specs=VMEM,
        scratch_shapes=[pltpu.VMEM(x.shape, x.dtype) for x in partials]
        + [pltpu.SemaphoreType.DMA((len(partials),))],
        cost_estimate=pl.CostEstimate(
            flops=len(partials) * tokens * width,
            transcendentals=0,
            bytes_accessed=4 * len(partials) * tokens * width,
        ),
        compiler_params=SMALL,
        name="round_query",
    )(*partials)


def merge(top, denom, numer, other_top, other_denom, other_numer):
    new_top = jnp.maximum(top, other_top)
    keep = jnp.exp2((top - new_top) * (HD**-0.5 * LOG2E))
    weight = jnp.exp2((other_top - new_top) * (HD**-0.5 * LOG2E))
    return new_top, denom * keep + other_denom * weight, numer * keep + other_numer * weight


def read_state(ref, part=slice(None)):
    if ref.dtype == jnp.bfloat16:
        parts = ref[HD:, part].astype(jnp.float32)
        top, denom = (parts[n : n + 1] + parts[n + 1 : n + 2] + parts[n + 2 : n + 3] for n in (0, 3))
        return top, denom, ref[:HD, part].astype(jnp.float32)
    return ref[HD : HD + 1, part], ref[HD + 8 : HD + 9, part], ref[:HD, part]


def exact_parts(x):
    high = x.astype(jnp.bfloat16).astype(jnp.float32)
    middle = (x - high).astype(jnp.bfloat16).astype(jnp.float32)
    return high, middle, x - high - middle


def attend(queries, chunks, steps, state, positions, lengths, seq_count, pairs, send=False):
    first = state is None
    tokens = positions.shape[1]
    columns = queries[0].shape[0]
    n_query = len(queries)
    n_chunks = len(chunks)
    keys_here = chunks[0].shape[-2]
    moved = [*queries, *chunks]
    inputs = [lengths, positions, *moved] + ([] if first else [state])

    def kernel(*refs):
        lengths_ref, positions_ref = refs[:2]
        moved_refs = refs[2 : 2 + len(moved)]
        out = refs[len(inputs)]
        held = refs[len(inputs) + 1 + send : -1]
        sem = refs[-1]
        copies = [
            pltpu.make_async_copy(src, dst, sem.at[n]) for n, (src, dst) in enumerate(zip(moved_refs, held))
        ]
        for copy in copies:
            copy.start()
        me = lax.axis_index("seq")
        other = swapped(me, pairs)
        limit = jnp.minimum(positions_ref[...], lengths_ref[0] - 1)
        limit = jnp.concatenate([limit] * (columns // tokens), axis=1)
        rows = lax.broadcasted_iota(jnp.int32, (keys_here, columns), 0)
        for copy in copies[:n_query]:
            copy.wait()
        q = held[0][...]
        if n_query == 2:
            q = jnp.where(other == me, q, held[1][...])
        for copy in copies[n_query:]:
            copy.wait()
        wide, deep = min(columns, 256), min(keys_here, 128)
        for c in range(0, columns, wide):
            part = slice(c, c + wide)
            sums = None if first else read_state(refs[len(inputs) - 1], part)
            for n, step in enumerate(steps):
                start = source(other, seq_count, step) * keys_here
                ref = held[n_query + n]
                scores = []
                for r in range(0, keys_here, deep):
                    score = lax.dot_general(
                        ref[0, r : r + deep],
                        q[part],
                        (((1,), (1,)), ((), ())),
                        preferred_element_type=jnp.float32,
                    )
                    scores.append(jnp.where(rows[:deep, part] <= limit[:, part] - (start + r), score, NONE_VISIBLE))
                block_max = functools.reduce(
                    jnp.maximum, [jnp.max(score, axis=0, keepdims=True) for score in scores]
                )
                block_total, block_sum = 0.0, 0.0
                for r, score in zip(range(0, keys_here, deep), scores):
                    expo = jnp.exp2((score - block_max) * (HD**-0.5 * LOG2E))
                    block_total = block_total + jnp.sum(expo, axis=0, keepdims=True)
                    block_sum = block_sum + lax.dot_general(
                        ref[1, r : r + deep],
                        expo.astype(jnp.bfloat16),
                        (((0,), (0,)), ((), ())),
                        preferred_element_type=jnp.float32,
                    )
                block_sum = block_sum.astype(jnp.bfloat16).astype(jnp.float32)
                block = block_max, block_total, block_sum
                sums = block if sums is None else merge(*sums, *block)
            top, denom, numer = sums
            out[:HD, part] = numer
            out[HD : HD + 8, part] = jnp.broadcast_to(top, (8, wide))
            out[HD + 8 :, part] = jnp.broadcast_to(denom, (8, wide))
            if send:
                sent = refs[len(inputs) + 1]
                sent[:HD, part] = numer.astype(jnp.bfloat16)
                parts = jnp.concatenate([*exact_parts(top), *exact_parts(denom), jnp.zeros((10, wide))], axis=0)
                sent[HD:, part] = parts.astype(jnp.bfloat16)

    return pl.pallas_call(
        kernel,
        out_shape=[
            jax.ShapeDtypeStruct((HD + 16, columns), dtype) for dtype in (jnp.float32, jnp.bfloat16)[: 1 + send]
        ],
        in_specs=[SMEM, VMEM] + [ANY] * len(moved) + [VMEM] * (len(inputs) - 2 - len(moved)),
        out_specs=[VMEM] * (1 + send),
        scratch_shapes=[pltpu.VMEM(x.shape, x.dtype) for x in moved]
        + [pltpu.SemaphoreType.DMA((len(moved),))],
        cost_estimate=pl.CostEstimate(
            flops=4 * n_chunks * keys_here * columns * HD,
            transcendentals=n_chunks * keys_here * columns,
            bytes_accessed=n_chunks * 4 * keys_here * HD,
        ),
        compiler_params=SMALL,
        name="attend",
    )(*inputs)


def finish(near, far, received, tokens, pairs):
    columns = near.shape[1]
    group = columns // tokens

    def kernel(near_ref, far_ref, received_ref, out):
        me = lax.axis_index("seq")
        mine = swapped(me, pairs) == me
        far_sums = [
            jnp.where(mine, one, two) for one, two in zip(read_state(far_ref), read_state(received_ref))
        ]
        _, denom, numer = merge(*read_state(near_ref), *far_sums)
        result = numer / denom
        for h in range(group):
            part = result[:, h * tokens : (h + 1) * tokens]
            out[:, h * HD : (h + 1) * HD] = jnp.transpose(part).astype(jnp.bfloat16)

    return pl.pallas_call(
        kernel,
        out_shape=jax.ShapeDtypeStruct((tokens, group * HD), jnp.bfloat16),
        in_specs=[VMEM] * 3,
        out_specs=VMEM,
        cost_estimate=pl.CostEstimate(
            flops=8 * HD * columns, transcendentals=0, bytes_accessed=12 * HD * columns
        ),
        compiler_params=SMALL,
        name="finish",
    )(near, far, received)


def partner_pairs(count):
    half = count // 2
    across = half + half // 2
    return [(one, one ^ across) for one in range(half // 2, half)][:PARTNERS]


def own_heads(inputs, w_query, cache_keys, cache_values, lengths, positions):
    seq_count = lax.axis_size("seq")
    batch_count = lax.axis_size("batch")
    half = seq_count // 2
    order = seq_order(seq_count)
    pairs = partner_pairs(seq_count)
    swap = dict([*pairs, *((two, one) for one, two in pairs)])
    meet = [(one, swap.get(one, one ^ 1)) for one in range(seq_count)]
    key_rows, value_rows, tokens = (
        pltpu.with_memory_space_constraint(x[0], pltpu.HBM) for x in (cache_keys, cache_values, inputs)
    )
    packed = pack(key_rows, value_rows, tokens, seq_count, batch_count, order[:1])
    packed, blocks = packed[:1], packed[1:]
    packed += pack(key_rows, value_rows, None, seq_count, batch_count, [*order[1:], 0])
    moved = {0: packed[-1]}
    for step, block in zip(order, packed):
        to = peers(seq_count, step)
        if step >= half:
            to = [(a, swap.get(b, b)) for a, b in to]
        moved[step] = lax.ppermute(block, "seq", to)
    halves, other_halves = [], []
    for step in range(1, batch_count):
        halves.append(lax.ppermute(blocks[step], "batch", peers(batch_count, step)))
        other_halves.append(lax.ppermute(halves[-1], "seq", peers(seq_count, 1)))
    partials = project(blocks[0], halves, other_halves, w_query)
    back = [partials[0]]
    for step in range(1, batch_count):
        back.append(lax.ppermute(partials[step], "batch", [(b, a) for a, b in peers(batch_count, step)]))
    query = round_query(back)
    queries = [query]
    if pairs:
        queries.append(lax.ppermute(query, "seq", meet))
    attend_ = functools.partial(attend, positions=positions, lengths=lengths, seq_count=seq_count)
    early, far_steps = [*range(half)], [s for s in order if s >= half]
    near = None
    for steps in (early[:-1], early[-1:]):
        (near,) = attend_([query], [moved[s] for s in steps], steps, near, pairs=[])
    far = attend_(queries, [moved[s] for s in far_steps], far_steps, None, pairs=pairs, send=bool(pairs))
    received = far[0]
    if pairs:
        received = lax.ppermute(far[1], "seq", meet)
    return finish(near, far[0], received, positions.shape[1], pairs)[None]


def split_positions(inputs, w_query, cache_keys, cache_values, lengths, positions):
    seq_count = lax.axis_size("seq")
    heads_here = H // seq_count
    group = H // KVH
    keys_here = cache_keys.shape[1]
    tokens = inputs[0]
    query_rows = tokens.shape[0]
    features = lax.all_to_all(inputs, "batch", split_axis=2, concat_axis=0, tiled=True)
    query = lax.psum_scatter(
        jnp.einsum("sqd,dc->sqc", features, w_query, preferred_element_type=jnp.float32),
        "batch",
        scatter_dimension=0,
        tiled=True,
    )[0]
    query = query.astype(jnp.bfloat16)
    all_query = lax.all_gather(query, "seq", axis=1, tiled=True)
    query_heads = all_query.reshape(query_rows, KVH, group, HD)
    key_pos = lax.axis_index("seq") * keys_here + jnp.arange(keys_here, dtype=jnp.int32)
    visible = (key_pos[None, :] <= positions[0][:, None]) & (key_pos[None, :] < lengths[0])
    key_rows = cache_keys[0]
    value_rows = cache_values[0]

    def one_head(kv_head):
        key_block = lax.dynamic_slice_in_dim(key_rows, kv_head * HD, HD, 1)
        value_block = lax.dynamic_slice_in_dim(value_rows, kv_head * HD, HD, 1)
        query_group = lax.dynamic_index_in_dim(query_heads, kv_head, 1, keepdims=False)
        score = jnp.einsum(
            "qrd,kd->rqk", query_group, key_block, preferred_element_type=jnp.float32
        ) * HD ** (-0.5)
        block_max = jnp.max(jnp.where(visible[None], score, -1e30), axis=-1)
        expo = jnp.where(visible[None], jnp.exp(score - block_max[..., None]), 0.0)
        block_total = jnp.sum(expo, axis=-1)
        prob = expo.astype(jnp.bfloat16)
        block_sum = jnp.einsum(
            "rqk,kd->rqd", prob, value_block, preferred_element_type=jnp.float32
        ).astype(jnp.bfloat16)
        return (block_sum, block_max, block_total)

    sums, maxima, totals = lax.map(one_head, jnp.arange(KVH, dtype=jnp.int32))
    sums = sums.reshape(1, H, query_rows, HD)
    maxima = maxima.reshape(1, H, query_rows)
    totals = totals.reshape(1, H, query_rows)
    got_sums = lax.all_to_all(sums, "seq", split_axis=1, concat_axis=0, tiled=True)
    got_max, got_total = (
        lax.all_to_all(maxima, "seq", split_axis=1, concat_axis=0, tiled=True),
        lax.all_to_all(totals, "seq", split_axis=1, concat_axis=0, tiled=True),
    )
    top = jnp.max(got_max, axis=0)
    weight = jnp.exp(got_max - top[None])
    numer = jnp.sum(weight[..., None] * got_sums.astype(jnp.float32), axis=0)
    denom = jnp.sum(weight * got_total, axis=0)
    result = numer / denom[..., None]
    return (
        jnp.transpose(result, (1, 0, 2))
        .reshape(query_rows, heads_here * HD)[None]
        .astype(jnp.bfloat16)
    )


def solution(mesh):
    in_specs = (
        P("batch", None, None),
        P("batch", "seq"),
        P("batch", "seq", None),
        P("batch", "seq", None),
        P("batch"),
        P("batch", None),
    )
    out_specs = P("batch", None, "seq")
    split = functools.partial(
        jax.shard_map, mesh=mesh, in_specs=in_specs, out_specs=out_specs, check_vma=False
    )
    if mesh.shape["seq"] != KVH:
        return split(split_positions)
    return split(own_heads)
```

```python
import functools

import jax
import jax.numpy as jnp
from jax import lax
from jax.experimental import pallas as pl
from jax.experimental.pallas import tpu as pltpu
from jax.sharding import PartitionSpec as P


H = 64
KVH = 8
HD = 128


ANY = pl.BlockSpec(memory_space=pl.ANY)
HBM = pl.BlockSpec(memory_space=pltpu.HBM)
VMEM = pl.BlockSpec(memory_space=pltpu.VMEM)
SMEM = pl.BlockSpec(memory_space=pltpu.SMEM)
PARTNERS = 2
SMALL = pltpu.CompilerParams(vmem_limit_bytes=24 << 20)
LOG2E = 1.4426950408889634
NONE_VISIBLE = -1e30


def peers(count, step):
    if count & (count - 1) == 0:
        return [(j, j ^ step) for j in range(count)]
    return [(j, (j + step) % count) for j in range(count)]


def target(me, count, step):
    return me ^ step if count & (count - 1) == 0 else lax.rem(me + step, count)


def source(me, count, step):
    return me ^ step if count & (count - 1) == 0 else lax.rem(me + count - step, count)


def seq_order(count):
    half = count // 2
    far = [*range(half + 2, count, 2), *range(half + 1, count, 2)]
    return [half, *range(2, half), *far, 1]


def pack(key_rows, value_rows, tokens, seq_count, batch_count, steps):
    keys_here, width = key_rows.shape
    share = width // seq_count
    sources = [key_rows, value_rows] + ([] if tokens is None else [tokens])
    shapes = [jax.ShapeDtypeStruct((2, keys_here, share), key_rows.dtype)] * len(steps)
    if tokens is not None:
        depth = tokens.shape[1] // batch_count
        widths = [depth] + [depth // 2] * (batch_count - 1)
        shapes = shapes + [jax.ShapeDtypeStruct((tokens.shape[0], width), tokens.dtype) for width in widths]

    def kernel(*refs):
        ins, outs, sem = refs[: len(sources)], refs[len(sources) : -1], refs[-1]
        copies = []

        def move(ref, start, size, out):
            columns = pl.ds(pl.multiple_of(start, HD), size)
            copy = pltpu.make_async_copy(ref.at[:, columns], out, sem.at[len(copies)])
            copy.start()
            copies.append(copy)

        if tokens is not None:
            me, half = lax.axis_index("batch"), lax.rem(lax.axis_index("seq"), 2)
            for step, width in enumerate(widths):
                start = target(me, batch_count, step) * depth + (half * width if step else 0)
                move(ins[2], start, width, outs[len(steps) + step])
        me = lax.axis_index("seq")
        for n, step in enumerate(steps):
            for part in range(2):
                move(ins[part], target(me, seq_count, step) * share, share, outs[n].at[part])
        for copy in copies:
            copy.wait()

    n_copies = 2 * len(steps) + (0 if tokens is None else batch_count)
    out = pl.pallas_call(
        kernel,
        out_shape=shapes,
        in_specs=[HBM] * len(sources),
        out_specs=[VMEM] * len(shapes),
        scratch_shapes=[pltpu.SemaphoreType.DMA((n_copies,))],
        cost_estimate=pl.CostEstimate(
            flops=0, transcendentals=0, bytes_accessed=len(steps) * 8 * keys_here * share
        ),
        compiler_params=SMALL,
    )(*sources)
    return list(out)


def project(own, halves, other_halves, weight):
    count = 1 + len(halves)
    rows, depth = own.shape
    columns = weight.shape[1]
    tile = min(256, columns)

    def kernel(*refs):
        ins, w_ref, outs, stacked = refs[: 2 * count - 1], refs[2 * count - 1], refs[2 * count : -1], refs[-1]
        mine = lax.rem(lax.axis_index("seq"), 2)
        stacked[:rows, :] = ins[0][...]
        for n in range(1, count):
            for which, ref in ((mine, ins[n]), (1 - mine, ins[count - 1 + n])):
                start = pl.multiple_of(which * (depth // 2), HD)
                stacked[n * rows : (n + 1) * rows, pl.ds(start, depth // 2)] = ref[...]
        for j in range(0, columns, tile):
            part = slice(j, j + tile)
            product = jnp.dot(stacked[...], w_ref[:, part], preferred_element_type=jnp.float32)
            for n in range(count):
                outs[n][:, part] = product[n * rows : (n + 1) * rows]

    return pl.pallas_call(
        kernel,
        out_shape=[jax.ShapeDtypeStruct((rows, columns), jnp.float32)] * count,
        in_specs=[VMEM] * (2 * count),
        out_specs=[VMEM] * count,
        scratch_shapes=[pltpu.VMEM((count * rows, depth), own.dtype)],
        cost_estimate=pl.CostEstimate(
            flops=2 * count * rows * depth * columns,
            transcendentals=0,
            bytes_accessed=2 * depth * columns + 6 * count * rows * depth,
        ),
        compiler_params=SMALL,
        name="project",
    )(own, *halves, *other_halves, weight)


def swapped(me, pairs):
    other = me
    for one, two in pairs:
        other = jnp.where(me == one, two, jnp.where(me == two, one, other))
    return other


def round_query(partials):
    tokens, width = partials[0].shape
    group = width // HD

    def kernel(*refs):
        held, out = refs[:-1], refs[-1]
        for h in range(group):
            head = slice(h * HD, (h + 1) * HD)
            total = held[0][:, head]
            for ref in held[1:]:
                total = total + ref[:, head]
            out[h * tokens : (h + 1) * tokens, :] = total.astype(jnp.bfloat16)

    return pl.pallas_call(
        kernel,
        out_shape=jax.ShapeDtypeStruct((group * tokens, HD), jnp.bfloat16),
        in_specs=[VMEM] * len(partials),
        out_specs=VMEM,
        cost_estimate=pl.CostEstimate(
            flops=len(partials) * tokens * width,
            transcendentals=0,
            bytes_accessed=4 * len(partials) * tokens * width,
        ),
        compiler_params=SMALL,
        name="round_query",
    )(*partials)


def merge(top, denom, numer, other_top, other_denom, other_numer):
    new_top = jnp.maximum(top, other_top)
    keep = jnp.exp2((top - new_top) * (HD**-0.5 * LOG2E))
    weight = jnp.exp2((other_top - new_top) * (HD**-0.5 * LOG2E))
    return new_top, denom * keep + other_denom * weight, numer * keep + other_numer * weight


def read_state(ref, part=slice(None)):
    if ref.dtype == jnp.bfloat16:
        parts = ref[HD:, part].astype(jnp.float32)
        top, denom = (parts[n : n + 1] + parts[n + 1 : n + 2] + parts[n + 2 : n + 3] for n in (0, 3))
        return top, denom, ref[:HD, part].astype(jnp.float32)
    return ref[HD : HD + 1, part], ref[HD + 8 : HD + 9, part], ref[:HD, part]


def exact_parts(x):
    high = x.astype(jnp.bfloat16).astype(jnp.float32)
    middle = (x - high).astype(jnp.bfloat16).astype(jnp.float32)
    return high, middle, x - high - middle


def attend(queries, chunks, steps, state, positions, lengths, seq_count, pairs, send=False):
    first = state is None
    tokens = positions.shape[1]
    columns = queries[0].shape[0]
    n_query = len(queries)
    n_chunks = len(chunks)
    keys_here = chunks[0].shape[-2]
    moved = [*queries, *chunks]
    inputs = [lengths, positions, *moved] + ([] if first else [state])

    def kernel(*refs):
        lengths_ref, positions_ref = refs[:2]
        moved_refs = refs[2 : 2 + len(moved)]
        out = refs[len(inputs)]
        held = moved_refs
        me = lax.axis_index("seq")
        other = swapped(me, pairs)
        limit = jnp.minimum(positions_ref[...], lengths_ref[0] - 1)
        limit = jnp.concatenate([limit] * (columns // tokens), axis=1)
        rows = lax.broadcasted_iota(jnp.int32, (keys_here, columns), 0)
        q = held[0][...]
        if n_query == 2:
            q = jnp.where(other == me, q, held[1][...])
        wide, deep = min(columns, 256), min(keys_here, 128)
        for c in range(0, columns, wide):
            part = slice(c, c + wide)
            sums = None if first else read_state(refs[len(inputs) - 1], part)
            for n, step in enumerate(steps):
                start = source(other, seq_count, step) * keys_here
                ref = held[n_query + n]
                scores = []
                for r in range(0, keys_here, deep):
                    score = lax.dot_general(
                        ref[0, r : r + deep],
                        q[part],
                        (((1,), (1,)), ((), ())),
                        preferred_element_type=jnp.float32,
                    )
                    scores.append(jnp.where(rows[:deep, part] <= limit[:, part] - (start + r), score, NONE_VISIBLE))
                block_max = functools.reduce(
                    jnp.maximum, [jnp.max(score, axis=0, keepdims=True) for score in scores]
                )
                block_total, block_sum = 0.0, 0.0
                for r, score in zip(range(0, keys_here, deep), scores):
                    expo = jnp.exp2((score - block_max) * (HD**-0.5 * LOG2E))
                    block_total = block_total + jnp.sum(expo, axis=0, keepdims=True)
                    block_sum = block_sum + lax.dot_general(
                        ref[1, r : r + deep],
                        expo.astype(jnp.bfloat16),
                        (((0,), (0,)), ((), ())),
                        preferred_element_type=jnp.float32,
                    )
                block_sum = block_sum.astype(jnp.bfloat16).astype(jnp.float32)
                block = block_max, block_total, block_sum
                sums = block if sums is None else merge(*sums, *block)
            top, denom, numer = sums
            out[:HD, part] = numer
            out[HD : HD + 8, part] = jnp.broadcast_to(top, (8, wide))
            out[HD + 8 :, part] = jnp.broadcast_to(denom, (8, wide))
            if send:
                sent = refs[len(inputs) + 1]
                sent[:HD, part] = numer.astype(jnp.bfloat16)
                parts = jnp.concatenate([*exact_parts(top), *exact_parts(denom), jnp.zeros((10, wide))], axis=0)
                sent[HD:, part] = parts.astype(jnp.bfloat16)

    return pl.pallas_call(
        kernel,
        out_shape=[
            jax.ShapeDtypeStruct((HD + 16, columns), dtype) for dtype in (jnp.float32, jnp.bfloat16)[: 1 + send]
        ],
        in_specs=[SMEM] + [VMEM] * (len(inputs) - 1),
        out_specs=[VMEM] * (1 + send),
        cost_estimate=pl.CostEstimate(
            flops=4 * n_chunks * keys_here * columns * HD,
            transcendentals=n_chunks * keys_here * columns,
            bytes_accessed=n_chunks * 4 * keys_here * HD,
        ),
        compiler_params=SMALL,
        name="attend",
    )(*inputs)


def finish(near, far, received, tokens, pairs):
    columns = near.shape[1]
    group = columns // tokens

    def kernel(near_ref, far_ref, received_ref, out, held, sem):
        me = lax.axis_index("seq")
        mine = swapped(me, pairs) == me
        wide = 2 * tokens
        copies = []
        for n in range(0, group, 2):
            part = slice(n * tokens, n * tokens + wide)
            far_sums = [
                jnp.where(mine, one, two)
                for one, two in zip(read_state(far_ref, part), read_state(received_ref, part))
            ]
            _, denom, numer = merge(*read_state(near_ref, part), *far_sums)
            result = jnp.transpose(numer * (1.0 / denom)).astype(jnp.bfloat16)
            for h in range(2):
                held[:, (n + h) * HD : (n + h + 1) * HD] = result[h * tokens : (h + 1) * tokens]
            columns_here = slice(n * HD, (n + 2) * HD)
            copy = pltpu.make_async_copy(held.at[:, columns_here], out.at[:, columns_here], sem.at[n // 2])
            copy.start()
            copies.append(copy)
        for copy in copies:
            copy.wait()

    return pl.pallas_call(
        kernel,
        out_shape=jax.ShapeDtypeStruct((tokens, group * HD), jnp.bfloat16),
        in_specs=[VMEM] * 3,
        out_specs=HBM,
        scratch_shapes=[
            pltpu.VMEM((tokens, group * HD), jnp.bfloat16),
            pltpu.SemaphoreType.DMA((group // 2,)),
        ],
        cost_estimate=pl.CostEstimate(
            flops=8 * HD * columns, transcendentals=0, bytes_accessed=12 * HD * columns
        ),
        compiler_params=SMALL,
        name="finish",
    )(near, far, received)


def partner_pairs(count):
    half = count // 2
    across = half + half // 2
    return [(one, one ^ across) for one in range(half // 2, half)][:PARTNERS]


def own_heads(inputs, w_query, cache_keys, cache_values, lengths, positions):
    seq_count = lax.axis_size("seq")
    batch_count = lax.axis_size("batch")
    half = seq_count // 2
    order = seq_order(seq_count)
    pairs = partner_pairs(seq_count)
    swap = dict([*pairs, *((two, one) for one, two in pairs)])
    meet = [(one, swap.get(one, one ^ 1)) for one in range(seq_count)]
    key_rows, value_rows, tokens = (
        pltpu.with_memory_space_constraint(x[0], pltpu.HBM) for x in (cache_keys, cache_values, inputs)
    )
    packed = pack(key_rows, value_rows, tokens, seq_count, batch_count, order[:1])
    packed, blocks = packed[:1], packed[1:]
    packed += pack(key_rows, value_rows, None, seq_count, batch_count, [*order[1:], 0])
    moved = {0: packed[-1]}
    for step, block in zip(order, packed):
        to = peers(seq_count, step)
        if step >= half:
            to = [(a, swap.get(b, b)) for a, b in to]
        moved[step] = lax.ppermute(block, "seq", to)
    halves, other_halves = [], []
    for step in range(1, batch_count):
        halves.append(lax.ppermute(blocks[step], "batch", peers(batch_count, step)))
        other_halves.append(lax.ppermute(halves[-1], "seq", peers(seq_count, 1)))
    partials = project(blocks[0], halves, other_halves, w_query)
    back = [partials[0]]
    for step in range(1, batch_count):
        back.append(lax.ppermute(partials[step], "batch", [(b, a) for a, b in peers(batch_count, step)]))
    query = round_query(back)
    queries = [query]
    if pairs:
        queries.append(lax.ppermute(query, "seq", meet))
    attend_ = functools.partial(attend, positions=positions, lengths=lengths, seq_count=seq_count)
    early, far_steps = [*range(half)], [s for s in order if s >= half]
    near = None
    for steps in (early[:-1], early[-1:]):
        (near,) = attend_([query], [moved[s] for s in steps], steps, near, pairs=[])
    far = attend_(queries, [moved[s] for s in far_steps], far_steps, None, pairs=pairs, send=bool(pairs))
    received = far[0]
    if pairs:
        received = lax.ppermute(far[1], "seq", meet)
    return finish(near, far[0], received, positions.shape[1], pairs)[None]


def split_positions(inputs, w_query, cache_keys, cache_values, lengths, positions):
    seq_count = lax.axis_size("seq")
    heads_here = H // seq_count
    group = H // KVH
    keys_here = cache_keys.shape[1]
    tokens = inputs[0]
    query_rows = tokens.shape[0]
    features = lax.all_to_all(inputs, "batch", split_axis=2, concat_axis=0, tiled=True)
    query = lax.psum_scatter(
        jnp.einsum("sqd,dc->sqc", features, w_query, preferred_element_type=jnp.float32),
        "batch",
        scatter_dimension=0,
        tiled=True,
    )[0]
    query = query.astype(jnp.bfloat16)
    all_query = lax.all_gather(query, "seq", axis=1, tiled=True)
    query_heads = all_query.reshape(query_rows, KVH, group, HD)
    key_pos = lax.axis_index("seq") * keys_here + jnp.arange(keys_here, dtype=jnp.int32)
    visible = (key_pos[None, :] <= positions[0][:, None]) & (key_pos[None, :] < lengths[0])
    key_rows = cache_keys[0]
    value_rows = cache_values[0]

    def one_head(kv_head):
        key_block = lax.dynamic_slice_in_dim(key_rows, kv_head * HD, HD, 1)
        value_block = lax.dynamic_slice_in_dim(value_rows, kv_head * HD, HD, 1)
        query_group = lax.dynamic_index_in_dim(query_heads, kv_head, 1, keepdims=False)
        score = jnp.einsum(
            "qrd,kd->rqk", query_group, key_block, preferred_element_type=jnp.float32
        ) * HD ** (-0.5)
        block_max = jnp.max(jnp.where(visible[None], score, -1e30), axis=-1)
        expo = jnp.where(visible[None], jnp.exp(score - block_max[..., None]), 0.0)
        block_total = jnp.sum(expo, axis=-1)
        prob = expo.astype(jnp.bfloat16)
        block_sum = jnp.einsum(
            "rqk,kd->rqd", prob, value_block, preferred_element_type=jnp.float32
        ).astype(jnp.bfloat16)
        return (block_sum, block_max, block_total)

    sums, maxima, totals = lax.map(one_head, jnp.arange(KVH, dtype=jnp.int32))
    sums = sums.reshape(1, H, query_rows, HD)
    maxima = maxima.reshape(1, H, query_rows)
    totals = totals.reshape(1, H, query_rows)
    got_sums = lax.all_to_all(sums, "seq", split_axis=1, concat_axis=0, tiled=True)
    got_max, got_total = (
        lax.all_to_all(maxima, "seq", split_axis=1, concat_axis=0, tiled=True),
        lax.all_to_all(totals, "seq", split_axis=1, concat_axis=0, tiled=True),
    )
    top = jnp.max(got_max, axis=0)
    weight = jnp.exp(got_max - top[None])
    numer = jnp.sum(weight[..., None] * got_sums.astype(jnp.float32), axis=0)
    denom = jnp.sum(weight * got_total, axis=0)
    result = numer / denom[..., None]
    return (
        jnp.transpose(result, (1, 0, 2))
        .reshape(query_rows, heads_here * HD)[None]
        .astype(jnp.bfloat16)
    )


def solution(mesh):
    in_specs = (
        P("batch", None, None),
        P("batch", "seq"),
        P("batch", "seq", None),
        P("batch", "seq", None),
        P("batch"),
        P("batch", None),
    )
    out_specs = P("batch", None, "seq")
    split = functools.partial(
        jax.shard_map, mesh=mesh, in_specs=in_specs, out_specs=out_specs, check_vma=False
    )
    if mesh.shape["seq"] != KVH:
        return split(split_positions)
    return split(own_heads)
```

```python
import functools

import jax
import jax.numpy as jnp
from jax import lax
from jax.experimental import pallas as pl
from jax.experimental.pallas import tpu as pltpu
from jax.sharding import PartitionSpec as P


H = 64
KVH = 8
HD = 128


ANY = pl.BlockSpec(memory_space=pl.ANY)
HBM = pl.BlockSpec(memory_space=pltpu.HBM)
VMEM = pl.BlockSpec(memory_space=pltpu.VMEM)
SMEM = pl.BlockSpec(memory_space=pltpu.SMEM)
PARTNERS = 2
FIRST = 2
SMALL = pltpu.CompilerParams(vmem_limit_bytes=24 << 20)
LOG2E = 1.4426950408889634
NONE_VISIBLE = -1e30


def peers(count, step):
    if count & (count - 1) == 0:
        return [(j, j ^ step) for j in range(count)]
    return [(j, (j + step) % count) for j in range(count)]


def target(me, count, step):
    return me ^ step if count & (count - 1) == 0 else lax.rem(me + step, count)


def source(me, count, step):
    return me ^ step if count & (count - 1) == 0 else lax.rem(me + count - step, count)


def seq_order(count):
    half = count // 2
    return [half, half + 1, *range(half + 2, count), *range(2, half), 1]


def pack(key_rows, value_rows, tokens, seq_count, batch_count, steps):
    keys_here, width = key_rows.shape
    share = width // seq_count
    sources = [key_rows, value_rows] + ([] if tokens is None else [tokens])
    shapes = [jax.ShapeDtypeStruct((2, keys_here, share), key_rows.dtype)] * len(steps)
    if tokens is not None:
        depth = tokens.shape[1] // batch_count
        widths = [depth] + [depth // 2] * (batch_count - 1)
        shapes = shapes + [jax.ShapeDtypeStruct((tokens.shape[0], width), tokens.dtype) for width in widths]

    def kernel(*refs):
        ins, outs, sem = refs[: len(sources)], refs[len(sources) : -1], refs[-1]
        copies = []

        def move(ref, start, size, out):
            columns = pl.ds(pl.multiple_of(start, HD), size)
            copy = pltpu.make_async_copy(ref.at[:, columns], out, sem.at[len(copies)])
            copy.start()
            copies.append(copy)

        if tokens is not None:
            me, half = lax.axis_index("batch"), lax.rem(lax.axis_index("seq"), 2)
            for step, width in enumerate(widths):
                start = target(me, batch_count, step) * depth + (half * width if step else 0)
                move(ins[2], start, width, outs[len(steps) + step])
        me = lax.axis_index("seq")
        for n, step in enumerate(steps):
            for part in range(2):
                move(ins[part], target(me, seq_count, step) * share, share, outs[n].at[part])
        for copy in copies:
            copy.wait()

    n_copies = 2 * len(steps) + (0 if tokens is None else batch_count)
    out = pl.pallas_call(
        kernel,
        out_shape=shapes,
        in_specs=[HBM] * len(sources),
        out_specs=[VMEM] * len(shapes),
        scratch_shapes=[pltpu.SemaphoreType.DMA((n_copies,))],
        cost_estimate=pl.CostEstimate(
            flops=0, transcendentals=0, bytes_accessed=len(steps) * 8 * keys_here * share
        ),
        compiler_params=SMALL,
    )(*sources)
    return list(out)


def project(own, halves, other_halves, weight):
    count = 1 + len(halves)
    rows, depth = own.shape
    columns = weight.shape[1]
    tile = min(256, columns)

    def kernel(*refs):
        ins, w_ref, outs, stacked = refs[: 2 * count - 1], refs[2 * count - 1], refs[2 * count : -1], refs[-1]
        mine = lax.rem(lax.axis_index("seq"), 2)
        stacked[:rows, :] = ins[0][...]
        for n in range(1, count):
            for which, ref in ((mine, ins[n]), (1 - mine, ins[count - 1 + n])):
                start = pl.multiple_of(which * (depth // 2), HD)
                stacked[n * rows : (n + 1) * rows, pl.ds(start, depth // 2)] = ref[...]
        for j in range(0, columns, tile):
            part = slice(j, j + tile)
            product = jnp.dot(stacked[...], w_ref[:, part], preferred_element_type=jnp.float32)
            for n in range(count):
                outs[n][:, part] = product[n * rows : (n + 1) * rows]

    return pl.pallas_call(
        kernel,
        out_shape=[jax.ShapeDtypeStruct((rows, columns), jnp.float32)] * count,
        in_specs=[VMEM] * (2 * count),
        out_specs=[VMEM] * count,
        scratch_shapes=[pltpu.VMEM((count * rows, depth), own.dtype)],
        cost_estimate=pl.CostEstimate(
            flops=2 * count * rows * depth * columns,
            transcendentals=0,
            bytes_accessed=2 * depth * columns + 6 * count * rows * depth,
        ),
        compiler_params=SMALL,
        name="project",
    )(own, *halves, *other_halves, weight)


def swapped(me, pairs):
    other = me
    for one, two in pairs:
        other = jnp.where(me == one, two, jnp.where(me == two, one, other))
    return other


def round_query(partials):
    tokens, width = partials[0].shape
    group = width // HD

    def kernel(*refs):
        held, outs = refs[:-2], refs[-2:]
        for h in range(group):
            head = slice(h * HD, (h + 1) * HD)
            total = held[0][:, head]
            for ref in held[1:]:
                total = total + ref[:, head]
            half, row = divmod(h, group // 2)
            outs[half][row * tokens : (row + 1) * tokens, :] = total.astype(jnp.bfloat16)

    return pl.pallas_call(
        kernel,
        out_shape=[jax.ShapeDtypeStruct((group // 2 * tokens, HD), jnp.bfloat16)] * 2,
        in_specs=[VMEM] * len(partials),
        out_specs=[VMEM] * 2,
        cost_estimate=pl.CostEstimate(
            flops=len(partials) * tokens * width,
            transcendentals=0,
            bytes_accessed=4 * len(partials) * tokens * width,
        ),
        compiler_params=SMALL,
        name="round_query",
    )(*partials)


def merge(top, denom, numer, other_top, other_denom, other_numer):
    new_top = jnp.maximum(top, other_top)
    keep = jnp.exp2((top - new_top) * (HD**-0.5 * LOG2E))
    weight = jnp.exp2((other_top - new_top) * (HD**-0.5 * LOG2E))
    return new_top, denom * keep + other_denom * weight, numer * keep + other_numer * weight


def read_state(ref, part=slice(None)):
    if ref.dtype == jnp.bfloat16:
        parts = ref[HD:, part].astype(jnp.float32)
        top, denom = (parts[n : n + 1] + parts[n + 1 : n + 2] + parts[n + 2 : n + 3] for n in (0, 3))
        return top, denom, ref[:HD, part].astype(jnp.float32)
    return ref[HD : HD + 1, part], ref[HD + 8 : HD + 9, part], ref[:HD, part]


def exact_parts(x):
    high = x.astype(jnp.bfloat16).astype(jnp.float32)
    middle = (x - high).astype(jnp.bfloat16).astype(jnp.float32)
    return high, middle, x - high - middle


def attend(own, met, chunks, steps, state, positions, lengths, seq_count, pairs, send=False):
    first = state is None
    tokens = positions.shape[1]
    wide = own[0].shape[0]
    columns = wide * len(own)
    n_chunks = len(chunks)
    keys_here = chunks[0].shape[-2]
    inputs = [lengths, positions, *own, *met, *chunks] + ([] if first else [state])

    def kernel(*refs):
        lengths_ref, positions_ref = refs[:2]
        own_refs, rest = refs[2 : 2 + len(own)], refs[2 + len(own) :]
        met_refs, chunk_refs = rest[: len(met)], rest[len(met) : len(met) + n_chunks]
        out = refs[len(inputs)]
        me = lax.axis_index("seq")
        other = swapped(me, pairs)
        limit = jnp.minimum(positions_ref[...], lengths_ref[0] - 1)
        limit = jnp.concatenate([limit] * (wide // tokens), axis=1)
        deep = min(keys_here, 128)
        rows = lax.broadcasted_iota(jnp.int32, (deep, wide), 0)
        for piece in range(len(own)):
            q = own_refs[piece][...]
            if met:
                q = jnp.where(other == me, q, met_refs[piece][...])
            part = slice(piece * wide, (piece + 1) * wide)
            sums = None if first else read_state(refs[len(inputs) - 1], part)
            for ref, step in zip(chunk_refs, steps):
                start = source(other, seq_count, step) * keys_here
                scores = []
                for r in range(0, keys_here, deep):
                    score = lax.dot_general(
                        ref[0, r : r + deep], q, (((1,), (1,)), ((), ())), preferred_element_type=jnp.float32
                    )
                    scores.append(jnp.where(rows <= limit - (start + r), score, NONE_VISIBLE))
                block_max = functools.reduce(
                    jnp.maximum, [jnp.max(score, axis=0, keepdims=True) for score in scores]
                )
                block_total, block_sum = 0.0, 0.0
                for r, score in zip(range(0, keys_here, deep), scores):
                    expo = jnp.exp2((score - block_max) * (HD**-0.5 * LOG2E))
                    block_total = block_total + jnp.sum(expo, axis=0, keepdims=True)
                    block_sum = block_sum + lax.dot_general(
                        ref[1, r : r + deep],
                        expo.astype(jnp.bfloat16),
                        (((0,), (0,)), ((), ())),
                        preferred_element_type=jnp.float32,
                    )
                block_sum = block_sum.astype(jnp.bfloat16).astype(jnp.float32)
                block = block_max, block_total, block_sum
                sums = block if sums is None else merge(*sums, *block)
            top, denom, numer = sums
            out[:HD, part] = numer
            out[HD : HD + 8, part] = jnp.broadcast_to(top, (8, wide))
            out[HD + 8 :, part] = jnp.broadcast_to(denom, (8, wide))
            if send:
                sent = refs[len(inputs) + 1]
                sent[:HD, part] = numer.astype(jnp.bfloat16)
                parts = jnp.concatenate([*exact_parts(top), *exact_parts(denom), jnp.zeros((10, wide))], axis=0)
                sent[HD:, part] = parts.astype(jnp.bfloat16)

    return pl.pallas_call(
        kernel,
        out_shape=[
            jax.ShapeDtypeStruct((HD + 16, columns), dtype) for dtype in (jnp.float32, jnp.bfloat16)[: 1 + send]
        ],
        in_specs=[SMEM] + [VMEM] * (len(inputs) - 1),
        out_specs=[VMEM] * (1 + send),
        cost_estimate=pl.CostEstimate(
            flops=4 * n_chunks * keys_here * columns * HD,
            transcendentals=n_chunks * keys_here * columns,
            bytes_accessed=n_chunks * 4 * keys_here * HD,
        ),
        compiler_params=SMALL,
        name="attend",
    )(*inputs)


def finish(near, far, received, tokens, pairs):
    columns = near.shape[1]
    group = columns // tokens

    def kernel(near_ref, *refs):
        far_refs, received_refs = refs[: len(far)], refs[len(far) : 2 * len(far)]
        out, held, sem = refs[2 * len(far) :]
        me = lax.axis_index("seq")
        mine = swapped(me, pairs) == me
        wide = 2 * tokens
        copies = []
        for n in range(0, group, 2):
            part = slice(n * tokens, n * tokens + wide)
            which, start = divmod(n * tokens, far[0].shape[1])
            inner = slice(start, start + wide)
            far_sums = [
                jnp.where(mine, one, two)
                for one, two in zip(
                    read_state(far_refs[which], inner), read_state(received_refs[which], inner)
                )
            ]
            _, denom, numer = merge(*read_state(near_ref, part), *far_sums)
            result = jnp.transpose(numer * (1.0 / denom)).astype(jnp.bfloat16)
            for h in range(2):
                held[:, (n + h) * HD : (n + h + 1) * HD] = result[h * tokens : (h + 1) * tokens]
            columns_here = slice(n * HD, (n + 2) * HD)
            copy = pltpu.make_async_copy(held.at[:, columns_here], out.at[:, columns_here], sem.at[n // 2])
            copy.start()
            copies.append(copy)
        for copy in copies:
            copy.wait()

    return pl.pallas_call(
        kernel,
        out_shape=jax.ShapeDtypeStruct((tokens, group * HD), jnp.bfloat16),
        in_specs=[VMEM] * (1 + 2 * len(far)),
        out_specs=HBM,
        scratch_shapes=[
            pltpu.VMEM((tokens, group * HD), jnp.bfloat16),
            pltpu.SemaphoreType.DMA((group // 2,)),
        ],
        cost_estimate=pl.CostEstimate(
            flops=8 * HD * columns, transcendentals=0, bytes_accessed=12 * HD * columns
        ),
        compiler_params=SMALL,
        name="finish",
    )(near, *far, *received)


def partner_pairs(count):
    half = count // 2
    across = half + half // 2
    return [(one, one ^ across) for one in range(half // 2, half)][:PARTNERS]


def own_heads(inputs, w_query, cache_keys, cache_values, lengths, positions):
    seq_count = lax.axis_size("seq")
    batch_count = lax.axis_size("batch")
    half = seq_count // 2
    order = seq_order(seq_count)
    pairs = partner_pairs(seq_count)
    swap = dict([*pairs, *((two, one) for one, two in pairs)])
    meet = [(one, swap.get(one, one ^ 1)) for one in range(seq_count)]
    key_rows, value_rows, tokens = (
        pltpu.with_memory_space_constraint(x[0], pltpu.HBM) for x in (cache_keys, cache_values, inputs)
    )
    packed = pack(key_rows, value_rows, tokens, seq_count, batch_count, order[:FIRST])
    packed, blocks = packed[:FIRST], packed[FIRST:]
    packed += pack(key_rows, value_rows, None, seq_count, batch_count, [*order[FIRST:], 0])
    moved = {0: packed[-1]}
    for step, block in zip(order, packed):
        to = peers(seq_count, step)
        if step >= half:
            to = [(a, swap.get(b, b)) for a, b in to]
        moved[step] = lax.ppermute(block, "seq", to)
    halves, other_halves = [], []
    for step in range(1, batch_count):
        halves.append(lax.ppermute(blocks[step], "batch", peers(batch_count, step)))
        other_halves.append(lax.ppermute(halves[-1], "seq", peers(seq_count, 1)))
    partials = project(blocks[0], halves, other_halves, w_query)
    back = [partials[0]]
    for step in range(1, batch_count):
        back.append(lax.ppermute(partials[step], "batch", [(b, a) for a, b in peers(batch_count, step)]))
    query = round_query(back)
    attend_ = functools.partial(attend, positions=positions, lengths=lengths, seq_count=seq_count)
    early, far_steps = [*range(half)], [s for s in order if s >= half]
    far, received = [], []
    for piece in query:
        met = lax.ppermute(piece, "seq", meet)
        sums, sent = attend_(
            [piece], [met], [moved[s] for s in far_steps], far_steps, None, pairs=pairs, send=True
        )
        received.append(lax.ppermute(sent, "seq", meet))
        far.append(sums)
    near = None
    for steps in (early[:-1], early[-1:]):
        (near,) = attend_(query, [], [moved[s] for s in steps], steps, near, pairs=[])
    return finish(near, far, received, positions.shape[1], pairs)[None]


def split_positions(inputs, w_query, cache_keys, cache_values, lengths, positions):
    seq_count = lax.axis_size("seq")
    heads_here = H // seq_count
    group = H // KVH
    keys_here = cache_keys.shape[1]
    tokens = inputs[0]
    query_rows = tokens.shape[0]
    features = lax.all_to_all(inputs, "batch", split_axis=2, concat_axis=0, tiled=True)
    query = lax.psum_scatter(
        jnp.einsum("sqd,dc->sqc", features, w_query, preferred_element_type=jnp.float32),
        "batch",
        scatter_dimension=0,
        tiled=True,
    )[0]
    query = query.astype(jnp.bfloat16)
    all_query = lax.all_gather(query, "seq", axis=1, tiled=True)
    query_heads = all_query.reshape(query_rows, KVH, group, HD)
    key_pos = lax.axis_index("seq") * keys_here + jnp.arange(keys_here, dtype=jnp.int32)
    visible = (key_pos[None, :] <= positions[0][:, None]) & (key_pos[None, :] < lengths[0])
    key_rows = cache_keys[0]
    value_rows = cache_values[0]

    def one_head(kv_head):
        key_block = lax.dynamic_slice_in_dim(key_rows, kv_head * HD, HD, 1)
        value_block = lax.dynamic_slice_in_dim(value_rows, kv_head * HD, HD, 1)
        query_group = lax.dynamic_index_in_dim(query_heads, kv_head, 1, keepdims=False)
        score = jnp.einsum(
            "qrd,kd->rqk", query_group, key_block, preferred_element_type=jnp.float32
        ) * HD ** (-0.5)
        block_max = jnp.max(jnp.where(visible[None], score, -1e30), axis=-1)
        expo = jnp.where(visible[None], jnp.exp(score - block_max[..., None]), 0.0)
        block_total = jnp.sum(expo, axis=-1)
        prob = expo.astype(jnp.bfloat16)
        block_sum = jnp.einsum(
            "rqk,kd->rqd", prob, value_block, preferred_element_type=jnp.float32
        ).astype(jnp.bfloat16)
        return (block_sum, block_max, block_total)

    sums, maxima, totals = lax.map(one_head, jnp.arange(KVH, dtype=jnp.int32))
    sums = sums.reshape(1, H, query_rows, HD)
    maxima = maxima.reshape(1, H, query_rows)
    totals = totals.reshape(1, H, query_rows)
    got_sums = lax.all_to_all(sums, "seq", split_axis=1, concat_axis=0, tiled=True)
    got_max, got_total = (
        lax.all_to_all(maxima, "seq", split_axis=1, concat_axis=0, tiled=True),
        lax.all_to_all(totals, "seq", split_axis=1, concat_axis=0, tiled=True),
    )
    top = jnp.max(got_max, axis=0)
    weight = jnp.exp(got_max - top[None])
    numer = jnp.sum(weight[..., None] * got_sums.astype(jnp.float32), axis=0)
    denom = jnp.sum(weight * got_total, axis=0)
    result = numer / denom[..., None]
    return (
        jnp.transpose(result, (1, 0, 2))
        .reshape(query_rows, heads_here * HD)[None]
        .astype(jnp.bfloat16)
    )


def solution(mesh):
    in_specs = (
        P("batch", None, None),
        P("batch", "seq"),
        P("batch", "seq", None),
        P("batch", "seq", None),
        P("batch"),
        P("batch", None),
    )
    out_specs = P("batch", None, "seq")
    split = functools.partial(
        jax.shard_map, mesh=mesh, in_specs=in_specs, out_specs=out_specs, check_vma=False
    )
    if mesh.shape["seq"] != KVH:
        return split(split_positions)
    return split(own_heads)
```
